128 devices in a mesh: fsdp: 32 (over z, x, core), tensor: 4 (over y).
Axes of the slice: x: 4, y: 4, z: 4, core: 2. Of those that a mesh axis runs over, the one named last changes fastest.
Arguments:
- hidden: bfloat16 [512, 28672], P('tensor', 'fsdp'), may hold values from -6 to 6
- down_weight: bfloat16 [28672, 16384], P('fsdp', 'tensor'), may hold values from -0.03125 to 0.03125
- covariance: float32 [16384, 16384], P('tensor', 'fsdp'), as said below
- keep_index: int32 [32, 8], P('fsdp'), may hold values from -1 to 15, as said below
- start_basis: float32 [16384, 512], P('fsdp'), may hold values from -6 to 6
Outputs:
- mlp_out: bfloat16 [512, 16384], P('fsdp', 'tensor')
- new_covariance: float32 [16384, 16384], P('tensor', 'fsdp')
- first_basis: float32 [16384, 512], P(('tensor', 'fsdp'))
- final_basis: float32 [16384, 512], P('fsdp')
The draws below stay inside these ranges and needn't reach their ends.
Inputs may be any that keep to these rules, and one draw needn't show every extreme that they name: `keep_index`: row b lists first between 1 and 8 distinct positions of 0 to 15, then -1 in the remaining slots; in every draw some row lists 8 positions. covariance is exactly symmetric and positive definite.
All inputs are finite; a program needn't handle non-finite values.
Results may differ from the reference program's by a relative error of at most 0.0015.
Values may be sent and summed in bfloat16 or wider, within the bound.
A program may use at most 128 MiB of HBM per device.

```python
import math
import jax
import jax.numpy as jnp
from jax import lax

D = 16384
FF = 28672
TOK_DEV = 16
RANK = 512
TOKENS = 512
KEEP_MOST = 8
N_TENSOR = 4


def draw_covariance(key, part):
    key_noise = jax.random.fold_in(key, 11)
    key_scale = jax.random.fold_in(key, 12)
    row_index = jnp.arange(D, dtype=jnp.float32)
    level = D / TOKENS
    spread = 0.9 * level / math.sqrt(D)
    roughness = jnp.exp(jax.random.uniform(key_scale, (D,), jnp.float32) * math.log(2.0))
    noise_field = jax.random.normal(key_noise, (D, D), jnp.float32) * spread
    symmetric = (noise_field + noise_field.T) * 0.5
    diagonal = level * (2.0 + 4.0 * row_index / D) * roughness
    return (symmetric + jnp.diag(diagonal)).astype(jnp.float32)


def draw_keep_index(key, part):
    key_order = jax.random.fold_in(key, 21)
    key_divisor = jax.random.fold_in(key, 22)
    key_trim = jax.random.fold_in(key, 23)
    key_full = jax.random.fold_in(key, 24)
    blocks = TOKENS // TOK_DEV
    scores = jax.random.randint(key_order, (blocks, TOK_DEV), 0, 1 << 20) * TOK_DEV + jnp.arange(TOK_DEV, dtype=jnp.int32)[None, :]
    ordering = jnp.argsort(scores, axis=1, stable=True)[:, :KEEP_MOST].astype(jnp.int32)
    divisor = 1 + jax.random.randint(key_divisor, (blocks,), 0, 4)
    trimmed = jax.random.randint(key_trim, (blocks,), 0, 2)
    counts = jnp.maximum(1, KEEP_MOST // divisor - trimmed)
    full_block = jax.random.randint(key_full, (), 0, blocks)
    counts = jnp.where(jnp.arange(blocks) == full_block, KEEP_MOST, counts)
    slot_index = jnp.arange(KEEP_MOST, dtype=jnp.int32)
    return jnp.where(slot_index[None, :] < counts[:, None], ordering, -1).astype(jnp.int32)


def raised(entries, stream_key, source, target, shards_of, factor):
    def block_of(dim):
        return (jnp.arange(entries.shape[dim]) // (entries.shape[dim] // shards_of)).reshape((-1,) + (1,) * (entries.ndim - 1 - dim))

    one_side = jax.random.permutation(stream_key, shards_of)[block_of(target)]
    second = (block_of(target) + shards_of // 2) % shards_of
    return jnp.where((block_of(source) == one_side) | (block_of(source) == second), factor * entries, entries)


def level_of(rng, dims, split, smallest, high):
    loudness = 1.0
    for axis_at, blocks in split:
        heights = jax.random.uniform(jax.random.fold_in(jax.random.fold_in(rng, 6), axis_at), (blocks,), jnp.float32, smallest / len(split), high / len(split))
        loudness = loudness * jnp.repeat(jnp.exp(heights), dims[axis_at] // blocks).reshape((-1,) + (1,) * (len(dims) - 1 - axis_at))
    return loudness


def noise(key, shape, deviation, bound, cuts=(), kind=jnp.bfloat16):
    drawn = deviation * jax.random.normal(key, shape, jnp.float32)
    if cuts:
        drawn = drawn * level_of(key, shape, cuts, -0.22, 0.18)
    return jnp.clip(drawn, -bound, bound).astype(kind)


def bell_draw_with(own_key, dims, scale, most, split, heavy, kind=jnp.bfloat16):
    values = scale * jax.random.normal(own_key, dims, jnp.float32)
    if split:
        values = values * level_of(own_key, dims, split, -0.22, 0.18)
    return jnp.clip(raised(values, jax.random.fold_in(own_key, 3), *heavy), -most, most).astype(kind)


def setup_inputs(seed: int = 0) -> dict:
    streams_of = jax.random.split(jax.random.key(seed), 6)
    hidden = bell_draw_with(streams_of[0], (TOKENS, FF), 1.0, 6.0, ((0, 4), (1, 32)), (1, 0, 32, 2.75))
    down_weight = noise(streams_of[1], (FF, D), FF ** -0.5, 0.03125, ((0, 32), (1, 4)))
    covariance = draw_covariance(jax.random.fold_in(streams_of[5], 71), 0)
    keep_index = draw_keep_index(jax.random.fold_in(streams_of[5], 71), 0)
    start_basis = noise(streams_of[4], (D, RANK), 1.0, 6.0, ((0, 32),), jnp.float32)
    return dict(hidden=hidden, down_weight=down_weight, covariance=covariance, keep_index=keep_index, start_basis=start_basis)


def orthonormal(image_rows):
    gram_matrix = jnp.dot(image_rows.T.astype(jnp.float32), image_rows.astype(jnp.float32), precision=lax.Precision.HIGHEST, preferred_element_type=jnp.float32)
    lower_factor = jnp.linalg.cholesky(gram_matrix)
    return jax.scipy.linalg.solve_triangular(lower_factor, image_rows.T, lower=True).T

def reference(hidden, down_weight, covariance, keep_index, start_basis):
    mlp_out = jnp.dot(hidden.astype(jnp.float32), down_weight.astype(jnp.float32), preferred_element_type=jnp.float32).astype(jnp.bfloat16)
    positions = jnp.arange(TOK_DEV, dtype=jnp.int32)
    keep_mask = jnp.any(keep_index[:, :, None] == positions[None, None, :], axis=1).reshape(TOKENS)
    kept_rows = mlp_out * keep_mask[:, None].astype(jnp.bfloat16)
    kept_blocks = kept_rows.reshape(TOKENS, N_TENSOR, D // N_TENSOR).transpose(1, 0, 2)
    cov_blocks = covariance.reshape(N_TENSOR, D // N_TENSOR, D)

    def update_block(pieces):
        cov_piece, kept_piece = pieces
        update = lax.dot_general(kept_piece.astype(jnp.float32), kept_rows.astype(jnp.float32), (((0,), (0,)), ((), ())), preferred_element_type=jnp.float32)
        return cov_piece + update * (1.0 / TOKENS)
    new_covariance = lax.map(update_block, (cov_blocks, kept_blocks)).reshape(D, D)
    image_one = jnp.dot(new_covariance.astype(jnp.float32), start_basis.astype(jnp.float32), precision=lax.Precision.HIGHEST, preferred_element_type=jnp.float32)
    basis_one = orthonormal(image_one)
    first_basis = basis_one * math.sqrt(D)
    image_two = jnp.dot(new_covariance.astype(jnp.float32), basis_one.astype(jnp.float32), precision=lax.Precision.HIGHEST, preferred_element_type=jnp.float32)
    final_basis = orthonormal(image_two) * math.sqrt(D)
    return (mlp_out, new_covariance, first_basis, final_basis)
```

```python
import functools
import math

import jax
import jax.numpy as jnp
from jax import lax
from jax.experimental import pallas as pl
from jax.experimental.pallas import tpu as pltpu
from jax.sharding import PartitionSpec as P

D = 16384
TOK_DEV = 16
F32 = jnp.float32
BF16 = jnp.bfloat16
HIGH = lax.Precision.HIGH


def inverse_factor_kernel(gram_ref, out_ref, scaled, work, state):
    n = gram_ref.shape[0]
    rows = lax.broadcasted_iota(jnp.int32, (n, n), 0)
    cols = lax.broadcasted_iota(jnp.int32, (n, n), 1)
    gram = gram_ref[...]
    diagonal = jnp.where(rows == cols, gram, 0.0)
    col_scale = lax.rsqrt(jnp.sum(diagonal, axis=1, keepdims=True))
    row_scale = lax.rsqrt(jnp.sum(diagonal, axis=0, keepdims=True))
    scaled[...] = gram * col_scale * row_scale

    def half_lower(residual):
        return jnp.where(rows > cols, residual, jnp.where(rows == cols, 0.5 * residual, 0.0))

    def residual_of(x, precision):
        left = jnp.dot(x, scaled[...], precision=precision, preferred_element_type=F32)
        full = lax.dot_general(
            left, x, (((1,), (1,)), ((), ())), precision=precision, preferred_element_type=F32
        )
        return full - jnp.where(rows == cols, 1.0, 0.0)

    eye = jnp.where(rows == cols, 1.0, 0.0)
    work[...] = eye - half_lower(scaled[...] - eye)

    @pl.loop(0, 3)
    def _(step):
        x = work[...]
        residual = residual_of(x, None)
        work[...] = x - jnp.dot(half_lower(residual), x, preferred_element_type=F32)

    state[0] = 1.0

    def unfinished(step):
        error = state[0]
        return jnp.logical_and(step < 12, jnp.logical_not(error < 1e-5))

    def refine(step):
        x = work[...]
        residual = residual_of(x, HIGH)
        work[...] = x - jnp.dot(half_lower(residual), x, precision=HIGH, preferred_element_type=F32)
        state[0] = jnp.sum(residual * residual)
        return step + 1

    lax.while_loop(unfinished, refine, 0)

    @pl.when(jnp.logical_not(state[0] < 1e-5))
    def _():
        work[...] = eye

        @pl.loop(0, n)
        def _(j):
            here = cols[0:1] == j
            pivot_row = scaled[pl.ds(j, 1), :]
            pivot = lax.rsqrt(jnp.sum(jnp.where(here, pivot_row, 0.0), axis=1, keepdims=True))
            left = jnp.sum(jnp.where(cols == j, scaled[...], 0.0), axis=1, keepdims=True) * pivot
            left = jnp.where(rows[:, 0:1] > j, left, 0.0)
            own = work[pl.ds(j, 1), :] * pivot
            scaled[...] = scaled[...] - left * (pivot_row * pivot)
            work[...] = work[...] - left * own
            work[pl.ds(j, 1), :] = own

    out_ref[...] = work[...] * row_scale


def inverse_factor(gram):
    n = gram.shape[0]
    return pl.pallas_call(
        inverse_factor_kernel,
        out_shape=jax.ShapeDtypeStruct((n, n), F32),
        in_specs=[pl.BlockSpec(memory_space=pltpu.VMEM)],
        out_specs=pl.BlockSpec(memory_space=pltpu.VMEM),
        scratch_shapes=[pltpu.VMEM((n, n), F32), pltpu.VMEM((n, n), F32), pltpu.SMEM((1,), F32)],
        cost_estimate=pl.CostEstimate(flops=8_000_000_000, bytes_accessed=2 << 20, transcendentals=0),
        name="inverse_factor",
    )(gram)


def times_transpose(rows, factor, scale=1.0):
    out = lax.dot_general(
        rows, factor, (((1,), (1,)), ((), ())), precision=HIGH, preferred_element_type=F32
    )
    return out * scale if scale != 1.0 else out


def gram_of(rows):
    return lax.dot_general(
        rows, rows, (((0,), (0,)), ((), ())), precision=HIGH, preferred_element_type=F32
    )


def swap_axes(share, planes, group):
    perm = [
        ((z * group + r) * planes + t, (t * group + r) * planes + z)
        for z in range(planes)
        for r in range(group)
        for t in range(planes)
    ]
    return lax.ppermute(share, ("fsdp", "tensor"), perm)


def spread(share, planes, group):
    moved = swap_axes(share, planes, group)
    whole = lax.all_gather(moved, "fsdp", axis=0)
    rows, width = share.shape
    return whole.reshape(planes, group, rows, width).transpose(1, 0, 2, 3).reshape(-1, width)


def body(hidden, down_weight, covariance, keep_index, start_basis):
    fsdp_count = lax.axis_size("fsdp")
    planes = lax.axis_size("tensor")
    group = fsdp_count // planes
    total_tokens = TOK_DEV * fsdp_count
    quarter, block_width = covariance.shape
    share_rows = quarter // fsdp_count
    f = lax.axis_index("fsdp")
    t = lax.axis_index("tensor")
    root = math.sqrt(D)

    start_share = lax.dynamic_slice_in_dim(start_basis, t * share_rows, share_rows, 0)
    start_rows = spread(start_share, planes, group)

    all_hidden = lax.all_gather(hidden, "tensor", axis=0, tiled=True)
    mlp_out = lax.psum_scatter(
        jnp.dot(all_hidden, down_weight, preferred_element_type=F32),
        "fsdp",
        scatter_dimension=0,
        tiled=True,
    ).astype(BF16)
    listed = keep_index[0]
    positions = jnp.arange(mlp_out.shape[0], dtype=jnp.int32)
    chosen = (listed[:, None] == positions[None, :]).astype(BF16)
    kept = jnp.dot(chosen, mlp_out, preferred_element_type=F32).astype(BF16)
    kept_rows = lax.all_gather(kept, "fsdp", axis=0, tiled=True)
    own = lax.dynamic_slice_in_dim(kept_rows, f % group * block_width, block_width, 1)
    kept_cols = lax.psum(jnp.where(t == f // group, own, jnp.zeros_like(own)), "tensor")
    update = lax.dot_general(
        kept_rows, kept_cols, (((0,), (0,)), ((), ())), preferred_element_type=F32
    )
    new_covariance = covariance + update * (1.0 / total_tokens)

    def image_share(rows):
        partial = lax.dot_general(
            new_covariance, rows, (((0,), (0,)), ((), ())), precision=HIGH, preferred_element_type=F32
        )
        return lax.psum_scatter(partial, "tensor", scatter_dimension=0, tiled=True)

    image_one = image_share(start_rows)
    image_rows = spread(image_one, planes, group)
    inverse_one = inverse_factor(lax.psum(gram_of(image_one), ("fsdp", "tensor")))
    own_rows = lax.dynamic_slice_in_dim(image_rows, f * share_rows, share_rows, 0)
    first_basis = times_transpose(own_rows, inverse_one, root)
    image_two = times_transpose(image_share(image_rows), inverse_one)
    whole_two = lax.all_gather(image_two, "tensor", axis=0, tiled=True)
    inverse_two = inverse_factor(lax.psum(gram_of(image_two), ("fsdp", "tensor")))
    final_basis = times_transpose(whole_two, inverse_two, root)
    return (mlp_out, new_covariance, first_basis, final_basis)


def solution(mesh):
    placed = (
        P("tensor", "fsdp"),
        P("fsdp", "tensor"),
        P("tensor", "fsdp"),
        P("fsdp", None),
        P("fsdp", None),
    )
    return jax.shard_map(
        body,
        mesh=mesh,
        in_specs=placed,
        out_specs=(
            P("fsdp", "tensor"),
            P("tensor", "fsdp"),
            P(("tensor", "fsdp"), None),
            P("fsdp", None),
        ),
        check_vma=False,
    )
```

```python
import functools
import math

import jax
import jax.numpy as jnp
from jax import lax
from jax.experimental import pallas as pl
from jax.experimental.pallas import tpu as pltpu
from jax.sharding import PartitionSpec as P

D = 16384
TOK_DEV = 16
F32 = jnp.float32
BF16 = jnp.bfloat16
HIGH = lax.Precision.HIGH


def inverse_factor_kernel(gram_ref, out_ref, scaled, work, state):
    n = gram_ref.shape[0]
    rows = lax.broadcasted_iota(jnp.int32, (n, n), 0)
    cols = lax.broadcasted_iota(jnp.int32, (n, n), 1)
    gram = gram_ref[...]
    diagonal = jnp.where(rows == cols, gram, 0.0)
    col_scale = lax.rsqrt(jnp.sum(diagonal, axis=1, keepdims=True))
    row_scale = lax.rsqrt(jnp.sum(diagonal, axis=0, keepdims=True))
    scaled[...] = gram * col_scale * row_scale

    def half_lower(residual):
        return jnp.where(rows > cols, residual, jnp.where(rows == cols, 0.5 * residual, 0.0))

    def residual_of(x, precision):
        left = jnp.dot(x, scaled[...], precision=precision, preferred_element_type=F32)
        full = lax.dot_general(
            left, x, (((1,), (1,)), ((), ())), precision=precision, preferred_element_type=F32
        )
        return full - jnp.where(rows == cols, 1.0, 0.0)

    eye = jnp.where(rows == cols, 1.0, 0.0)
    work[...] = eye - half_lower(scaled[...] - eye)

    @pl.loop(0, 3)
    def _(step):
        x = work[...]
        residual = residual_of(x, None)
        work[...] = x - jnp.dot(half_lower(residual), x, preferred_element_type=F32)

    state[0] = 1.0

    def unfinished(step):
        error = state[0]
        return jnp.logical_and(step < 12, jnp.logical_not(error < 1e-5))

    def refine(step):
        x = work[...]
        residual = residual_of(x, HIGH)
        work[...] = x - jnp.dot(half_lower(residual), x, precision=HIGH, preferred_element_type=F32)
        state[0] = jnp.sum(residual * residual)
        return step + 1

    lax.while_loop(unfinished, refine, 0)

    @pl.when(jnp.logical_not(state[0] < 1e-5))
    def _():
        work[...] = eye

        @pl.loop(0, n)
        def _(j):
            here = cols[0:1] == j
            pivot_row = scaled[pl.ds(j, 1), :]
            pivot = lax.rsqrt(jnp.sum(jnp.where(here, pivot_row, 0.0), axis=1, keepdims=True))
            left = jnp.sum(jnp.where(cols == j, scaled[...], 0.0), axis=1, keepdims=True) * pivot
            left = jnp.where(rows[:, 0:1] > j, left, 0.0)
            own = work[pl.ds(j, 1), :] * pivot
            scaled[...] = scaled[...] - left * (pivot_row * pivot)
            work[...] = work[...] - left * own
            work[pl.ds(j, 1), :] = own

    out_ref[...] = work[...] * row_scale


def inverse_factor(gram):
    n = gram.shape[0]
    return pl.pallas_call(
        inverse_factor_kernel,
        out_shape=jax.ShapeDtypeStruct((n, n), F32),
        in_specs=[pl.BlockSpec(memory_space=pltpu.VMEM)],
        out_specs=pl.BlockSpec(memory_space=pltpu.VMEM),
        scratch_shapes=[pltpu.VMEM((n, n), F32), pltpu.VMEM((n, n), F32), pltpu.SMEM((1,), F32)],
        cost_estimate=pl.CostEstimate(flops=8_000_000_000, bytes_accessed=2 << 20, transcendentals=0),
        name="inverse_factor",
    )(gram)


def times_transpose(rows, factor, scale=1.0):
    out = lax.dot_general(
        rows, factor, (((1,), (1,)), ((), ())), precision=HIGH, preferred_element_type=F32
    )
    return out * scale if scale != 1.0 else out


def gram_of(rows):
    return lax.dot_general(
        rows, rows, (((0,), (0,)), ((), ())), precision=HIGH, preferred_element_type=F32
    )


MESH = pl.DeviceIdType.MESH
RING = 4


class Place:
    def __init__(self):
        f = lax.axis_index("fsdp")
        self.t = lax.axis_index("tensor")
        self.c = lax.rem(f, 2)
        self.x = lax.rem(lax.div(f, 2), RING)
        self.z = lax.div(f, 2 * RING)

    def along(self, axis, step):
        return lax.rem(getattr(self, axis) + (step + RING), RING)

    def device(self, **moved):
        at = {name: moved.get(name, getattr(self, name)) for name in ("z", "x", "c", "t")}
        return {"fsdp": (at["z"] * RING + at["x"]) * 2 + at["c"], "tensor": at["t"]}

    def ahead(self, axis, step):
        return self.device(**{axis: self.along(axis, step)})

    def other_core(self):
        return self.device(c=1 - self.c)


def meet(devices, place=None):
    barrier = pltpu.get_barrier_semaphore()
    for device in devices:
        pl.semaphore_signal(barrier, inc=1, device_id=device, device_id_type=MESH)
    count = len(devices)
    if place is not None:

        @pl.when(place.t != place.z)
        def _():
            pl.semaphore_signal(
                barrier, inc=1, device_id=place.device(z=place.t, t=place.z), device_id_type=MESH
            )

        count = count + jnp.where(place.t != place.z, 1, 0)
    pl.semaphore_wait(barrier, count)


class Links:
    def __init__(self, send, recv):
        self.send, self.recv, self.started = send, recv, []

    def copy(self, src, dst, device):
        i = len(self.started)
        made = pltpu.make_async_remote_copy(
            src_ref=src,
            dst_ref=dst,
            send_sem=self.send.at[i],
            recv_sem=self.recv.at[i],
            device_id=device,
            device_id_type=MESH,
        )
        self.started.append(made)
        return made

    def go(self, src, dst, device):
        made = self.copy(src, dst, device)
        made.start()
        return made


def gather_plane(own, out, slot, width, links, place):
    half, piece = width // 2, width // 4
    ways = ((0, "x", "z"), (1, "z", "x"))

    def at(z, x, cols):
        return out.at[slot(z, x, place.c) + (slice(None), cols)]

    def spot(axis, step, cols):
        z = place.along("z", step) if axis == "z" else place.z
        x = place.along("x", step) if axis == "x" else place.x
        return at(z, x, cols)

    def line(axis, other, step, cols):
        if axis == "x":
            return at(place.along(other, step), slice(None), cols)
        return at(slice(None), place.along(other, step), cols)

    def half_cols(h):
        return pl.ds(h * half, half)

    def piece_cols(h, d):
        return pl.ds(h * half + (0 if d > 0 else piece), piece)

    first, second, third, fourth, rest = {}, {}, {}, {}, []
    for h, axis, _ in ways:
        for d in (1, -1):
            cols = half_cols(h)
            first[h, d] = links.go(own.at[:, cols], spot(axis, 0, cols), place.ahead(axis, d))
    for h, axis, _ in ways:
        for d in (1, -1):
            first[h, d].wait_recv()
            cols = piece_cols(h, d)
            chunk = spot(axis, -d, cols)
            second[h, d] = links.go(chunk, chunk, place.ahead(axis, d))
    return ways, line, half_cols, piece_cols, second, third, fourth, rest


def finish_plane(parts, links, place):
    ways, line, half_cols, piece_cols, second, third, fourth, rest = parts
    for h, axis, other in ways:
        for d in (1, -1):
            second[h, d].wait_recv()
        whole = line(axis, other, 0, half_cols(h))
        for d in (1, -1):
            third[h, d] = links.go(whole, whole, place.ahead(other, d))
        rest.append(links.go(whole, whole, place.other_core()))
    for h, axis, other in ways:
        for d in (1, -1):
            third[h, d].wait_recv()
            part = line(axis, other, -d, piece_cols(h, d))
            fourth[h, d] = links.go(part, part, place.ahead(other, d))
            whole = line(axis, other, -d, half_cols(h))
            rest.append(links.go(whole, whole, place.other_core()))
    for h, axis, other in ways:
        for d in (1, -1):
            fourth[h, d].wait_recv()
            part = line(axis, other, -2 * d, piece_cols(h, d))
            rest.append(links.go(part, part, place.other_core()))
    for made in rest:
        made.wait_recv()


GATHER_COPIES = 26


def plane_neighbours(place):
    return [place.ahead(axis, d) for axis in ("x", "z") for d in (1, -1)] + [place.other_core()]


def by_column(z, x, c):
    return (x, c, z)


def by_token(z, x, c):
    return (z, x, c)


def swap_in(share, out, links, place, sem):
    sent = links.copy(
        share, out.at[by_column(place.t, place.x, place.c)], place.device(z=place.t, t=place.z)
    )

    @pl.when(place.t != place.z)
    def _():
        sent.start()
        sent.wait_recv()

    @pl.when(place.t == place.z)
    def _():
        kept = pltpu.make_async_copy(share, out.at[by_column(place.z, place.x, place.c)], sem)
        kept.start()
        kept.wait()

    return sent


def settle(links, place, swapped):
    for made in links.started:
        if made is swapped:

            @pl.when(place.t != place.z)
            def _():
                made.wait_send()
        else:
            made.wait_send()


def spread_kernel(share_ref, out_ref, send, recv, sem):
    place = Place()
    links = Links(send, recv)
    meet(plane_neighbours(place), place)
    swapped = swap_in(share_ref, out_ref, links, place, sem)
    own = out_ref.at[by_column(place.z, place.x, place.c)]
    parts = gather_plane(own, out_ref, by_column, share_ref.shape[1], links, place)
    finish_plane(parts, links, place)
    settle(links, place, swapped)


def spread(share, collective_id):
    rows, width = share.shape
    out = pl.pallas_call(
        spread_kernel,
        out_shape=jax.ShapeDtypeStruct((RING, 2, RING, rows, width), share.dtype),
        in_specs=[pl.BlockSpec(memory_space=pltpu.VMEM)],
        out_specs=pl.BlockSpec(memory_space=pl.ANY),
        scratch_shapes=[
            pltpu.SemaphoreType.DMA((GATHER_COPIES + 1,)),
            pltpu.SemaphoreType.DMA((GATHER_COPIES + 1,)),
            pltpu.SemaphoreType.DMA,
        ],
        compiler_params=pltpu.CompilerParams(collective_id=collective_id, has_side_effects=True),
        name="spread",
    )(share)
    return out.reshape(-1, width)


def reduce_y(part_ref, share_ref, relay, build, arrive, links, place):
    rows, width = share_ref.shape
    half = width // 2
    low, high = pl.ds(0, half), pl.ds(half, half)

    def quarter(step, cols):
        start = pl.multiple_of(place.along("t", step) * rows, rows)
        return part_ref.at[pl.ds(start, rows), cols]

    up, down = place.ahead("t", 1), place.ahead("t", -1)
    far_up = links.go(quarter(2, low), relay.at[0], up)
    far_down = links.go(quarter(2, high), relay.at[1], down)
    near_up = links.go(quarter(1, high), arrive.at[0, :, high], up)
    near_down = links.go(quarter(-1, low), arrive.at[1, :, low], down)
    far_up.wait_recv()
    build[0] = quarter(1, low)[...] + relay[0]
    sum_up = links.go(build.at[0], arrive.at[0, :, low], up)
    far_down.wait_recv()
    build[1] = quarter(-1, high)[...] + relay[1]
    sum_down = links.go(build.at[1], arrive.at[1, :, high], down)
    for made in (near_up, near_down, sum_up, sum_down):
        made.wait_recv()
    share_ref[...] = quarter(0, pl.ds(0, width))[...] + (arrive[0] + arrive[1])


REDUCE_COPIES = 6


def reduce_scratch(rows, width):
    return [
        pltpu.VMEM((2, rows, width // 2), F32),
        pltpu.VMEM((2, rows, width // 2), F32),
        pltpu.VMEM((2, rows, width), F32),
    ]


def y_neighbours(place):
    return [place.ahead("t", 1), place.ahead("t", -1)]


def reduce_kernel(part_ref, share_ref, relay, build, arrive, send, recv):
    place = Place()
    links = Links(send, recv)
    meet(y_neighbours(place))
    reduce_y(part_ref, share_ref, relay, build, arrive, links, place)
    for made in links.started:
        made.wait_send()


def reduce_over_y(part, collective_id):
    rows, width = part.shape[0] // RING, part.shape[1]
    return pl.pallas_call(
        reduce_kernel,
        out_shape=jax.ShapeDtypeStruct((rows, width), F32),
        in_specs=[pl.BlockSpec(memory_space=pltpu.VMEM)],
        out_specs=pl.BlockSpec(memory_space=pltpu.VMEM),
        scratch_shapes=reduce_scratch(rows, width)
        + [pltpu.SemaphoreType.DMA((REDUCE_COPIES,)), pltpu.SemaphoreType.DMA((REDUCE_COPIES,))],
        compiler_params=pltpu.CompilerParams(collective_id=collective_id, has_side_effects=True),
        name="reduce_over_y",
    )(part)


def reduce_spread_kernel(part_ref, share_ref, out_ref, relay, build, arrive, send, recv, sem):
    place = Place()
    links = Links(send, recv)
    meet(plane_neighbours(place) + y_neighbours(place), place)
    reduce_y(part_ref, share_ref, relay, build, arrive, links, place)
    swapped = swap_in(share_ref, out_ref, links, place, sem)
    own = out_ref.at[by_column(place.z, place.x, place.c)]
    parts = gather_plane(own, out_ref, by_column, share_ref.shape[1], links, place)
    finish_plane(parts, links, place)
    settle(links, place, swapped)


def reduce_and_spread(part, collective_id):
    rows, width = part.shape[0] // RING, part.shape[1]
    copies = REDUCE_COPIES + 1 + GATHER_COPIES
    share, out = pl.pallas_call(
        reduce_spread_kernel,
        out_shape=(
            jax.ShapeDtypeStruct((rows, width), F32),
            jax.ShapeDtypeStruct((RING, 2, RING, rows, width), F32),
        ),
        in_specs=[pl.BlockSpec(memory_space=pltpu.VMEM)],
        out_specs=(pl.BlockSpec(memory_space=pltpu.VMEM), pl.BlockSpec(memory_space=pl.ANY)),
        scratch_shapes=reduce_scratch(rows, width)
        + [
            pltpu.SemaphoreType.DMA((copies,)),
            pltpu.SemaphoreType.DMA((copies,)),
            pltpu.SemaphoreType.DMA,
        ],
        compiler_params=pltpu.CompilerParams(collective_id=collective_id, has_side_effects=True),
        name="reduce_and_spread",
    )(part)
    return share, out.reshape(-1, width)


def kept_kernel(kept_ref, rows_ref, cols_ref, send, recv, sem):
    place = Place()
    links = Links(send, recv)
    meet(plane_neighbours(place) + y_neighbours(place))
    local = pltpu.make_async_copy(kept_ref, rows_ref.at[by_token(place.z, place.x, place.c)], sem)
    local.start()
    parts = gather_plane(kept_ref, rows_ref, by_token, kept_ref.shape[1], links, place)
    local.wait()
    finish_plane(parts, links, place)
    for made in links.started:
        made.wait_send()
    width = cols_ref.shape[-1]
    start = pl.multiple_of((place.x * 2 + place.c) * width, width)
    source = rows_ref.at[:, :, :, :, pl.ds(start, width)]
    distance = lax.rem(place.t - place.z + RING, RING)
    up, down = place.ahead("t", 1), place.ahead("t", -1)
    to_up = links.copy(source, cols_ref, up)
    to_down = links.copy(source, cols_ref, down)
    low = cols_ref.at[pl.ds(0, RING // 2)]
    high = cols_ref.at[pl.ds(RING // 2, RING // 2)]
    on_up = links.copy(low, low, up)
    on_down = links.copy(high, high, down)

    @pl.when(distance == 0)
    def _():
        to_up.start()
        to_down.start()
        own = pltpu.make_async_copy(source, cols_ref, sem)
        own.start()
        own.wait()
        to_up.wait_send()
        to_down.wait_send()

    @pl.when(distance == 1)
    def _():
        to_up.wait_recv()
        on_up.start()
        on_up.wait_send()

    @pl.when(distance == 3)
    def _():
        to_down.wait_recv()
        on_down.start()
        on_down.wait_send()

    @pl.when(distance == 2)
    def _():
        on_up.wait_recv()
        on_down.wait_recv()


def gather_kept(kept, tile_width, collective_id):
    rows, width = kept.shape
    lead = (RING, RING, 2, rows)
    copies = GATHER_COPIES + 4
    kept_rows, kept_cols = pl.pallas_call(
        kept_kernel,
        out_shape=(
            jax.ShapeDtypeStruct(lead + (width,), kept.dtype),
            jax.ShapeDtypeStruct(lead + (tile_width,), kept.dtype),
        ),
        in_specs=[pl.BlockSpec(memory_space=pltpu.VMEM)],
        out_specs=(pl.BlockSpec(memory_space=pltpu.VMEM), pl.BlockSpec(memory_space=pltpu.VMEM)),
        scratch_shapes=[
            pltpu.SemaphoreType.DMA((copies,)),
            pltpu.SemaphoreType.DMA((copies,)),
            pltpu.SemaphoreType.DMA,
        ],
        compiler_params=pltpu.CompilerParams(collective_id=collective_id, has_side_effects=True),
        name="gather_kept",
    )(kept)
    return kept_rows.reshape(-1, width), kept_cols.reshape(-1, tile_width)


def total_kernel(with_rows, *refs):
    if with_rows:
        gram_ref, rows_ref, out_ref, all_ref = refs[:4]
        refs = refs[4:]
    else:
        gram_ref, out_ref = refs[:2]
        refs = refs[2:]
    pair, mine, first, second, last, sum_one, sum_two, send, recv = refs
    place = Place()
    links = Links(send, recv)
    n = gram_ref.shape[0]
    half, width = n // 2, n // 2
    block, piece = half // RING, half // RING // RING
    ways = (("x", "z", pl.ds(0, width)), ("z", "x", pl.ds(width, width)))
    meet(
        [place.other_core()]
        + [place.ahead(axis, k) for axis in ("x", "z", "t") for k in (1, 2, 3)]
    )
    kept_base = pl.multiple_of(place.c * half, half)
    gone_base = pl.multiple_of((1 - place.c) * half, half)
    swapped = links.go(gram_ref.at[pl.ds(gone_base, half)], pair, place.other_core())
    relayed = []
    if with_rows:
        around = all_ref.at[place.t]
        relayed = [links.go(rows_ref, around, place.ahead("t", d)) for d in (1, -1)]
        all_ref[pl.ds(place.t, 1)] = rows_ref[...][None]
    swapped.wait_recv()
    mine[...] = gram_ref[pl.ds(kept_base, half), :] + pair[...]
    sent = {}
    for p, (axis, other, cols) in enumerate(ways):
        for k in (1, 2, 3):
            start = pl.multiple_of(place.along(axis, k) * block, block)
            sent[p, k] = links.go(
                mine.at[pl.ds(start, block), cols], first.at[p, k - 1], place.ahead(axis, k)
            )
    for p, (axis, other, cols) in enumerate(ways):
        for k in (1, 2, 3):
            sent[p, k].wait_recv()
        start = pl.multiple_of(getattr(place, axis) * block, block)
        sum_one[p] = (mine[pl.ds(start, block), cols] + first[p, 0]) + (first[p, 1] + first[p, 2])
        for k in (1, 2, 3):
            start = pl.multiple_of(place.along(other, k) * piece, piece)
            sent[p, k] = links.go(
                sum_one.at[p, pl.ds(start, piece)], second.at[p, k - 1], place.ahead(other, k)
            )
    for p, (axis, other, cols) in enumerate(ways):
        for k in (1, 2, 3):
            sent[p, k].wait_recv()
        start = pl.multiple_of(getattr(place, other) * piece, piece)
        sum_two[p] = (sum_one[p, pl.ds(start, piece), :] + second[p, 0]) + (second[p, 1] + second[p, 2])
        for k in (1, 2, 3):
            sent[p, k] = links.go(sum_two.at[p], last.at[p, place.t], place.ahead("t", k))
        last[p, pl.ds(place.t, 1)] = sum_two[p][None]
    for p, (axis, other, cols) in enumerate(ways):
        for k in (1, 2, 3):
            sent[p, k].wait_recv()
        base = kept_base + getattr(place, axis) * block
        start = pl.multiple_of(base + getattr(place, other) * piece, piece)
        final = out_ref.at[pl.ds(start, piece), cols]
        final[...] = (last[p, 0] + last[p, 1]) + (last[p, 2] + last[p, 3])
        for k in (1, 2, 3):
            sent[p, k] = links.go(final, final, place.ahead(other, k))
    if with_rows:
        part = rows_ref.shape[0] // 2
        onward = []
        for d, made in zip((1, -1), relayed):
            made.wait_recv()
            held = all_ref.at[place.along("t", -d), pl.ds(0 if d > 0 else part, part)]
            onward.append(links.go(held, held, place.ahead("t", d)))
    for p, (axis, other, cols) in enumerate(ways):
        for k in (1, 2, 3):
            sent[p, k].wait_recv()
        start = pl.multiple_of(kept_base + getattr(place, axis) * block, block)
        whole = out_ref.at[pl.ds(start, block), cols]
        for k in (1, 2, 3):
            sent[p, k] = links.go(whole, whole, place.ahead(axis, k))
    for p in range(2):
        for k in (1, 2, 3):
            sent[p, k].wait_recv()
    side = out_ref.at[pl.ds(kept_base, half)]
    links.go(side, side, place.other_core()).wait_recv()
    if with_rows:
        for made in onward:
            made.wait_recv()
    for made in links.started:
        made.wait_send()


def total_gram(gram, collective_id, rows=None):
    n = gram.shape[0]
    block, piece = n // 2 // RING, n // 2 // RING // RING
    copies = 2 + 30 + (4 if rows is not None else 0)
    shapes = [jax.ShapeDtypeStruct((n, n), F32)]
    operands = [gram]
    if rows is not None:
        shapes.append(jax.ShapeDtypeStruct((RING,) + rows.shape, F32))
        operands.append(rows)
    vmem = pl.BlockSpec(memory_space=pltpu.VMEM)
    out = pl.pallas_call(
        functools.partial(total_kernel, rows is not None),
        out_shape=tuple(shapes),
        in_specs=[vmem] * len(operands),
        out_specs=tuple([vmem] * len(shapes)),
        scratch_shapes=[
            pltpu.VMEM((n // 2, n), F32),
            pltpu.VMEM((n // 2, n), F32),
            pltpu.VMEM((2, 3, block, n // 2), F32),
            pltpu.VMEM((2, 3, piece, n // 2), F32),
            pltpu.VMEM((2, RING, piece, n // 2), F32),
            pltpu.VMEM((2, block, n // 2), F32),
            pltpu.VMEM((2, piece, n // 2), F32),
            pltpu.SemaphoreType.DMA((copies,)),
            pltpu.SemaphoreType.DMA((copies,)),
        ],
        compiler_params=pltpu.CompilerParams(collective_id=collective_id, has_side_effects=True),
        name="total_gram",
    )(*operands)
    if rows is None:
        return out[0]
    return out[0], out[1].reshape(-1, rows.shape[1])


def body(hidden, down_weight, covariance, keep_index, start_basis):
    fsdp_count = lax.axis_size("fsdp")
    total_tokens = TOK_DEV * fsdp_count
    quarter, block_width = covariance.shape
    share_rows = quarter // fsdp_count
    f = lax.axis_index("fsdp")
    t = lax.axis_index("tensor")
    root = math.sqrt(D)

    start_share = lax.dynamic_slice_in_dim(start_basis, t * share_rows, share_rows, 0)
    start_rows = spread(start_share, 1)

    all_hidden = lax.all_gather(hidden, "tensor", axis=0, tiled=True)
    mlp_out = lax.psum_scatter(
        jnp.dot(all_hidden, down_weight, preferred_element_type=F32),
        "fsdp",
        scatter_dimension=0,
        tiled=True,
    ).astype(BF16)
    listed = keep_index[0]
    positions = jnp.arange(mlp_out.shape[0], dtype=jnp.int32)
    chosen = (listed[:, None] == positions[None, :]).astype(BF16)
    kept = jnp.dot(chosen, mlp_out, preferred_element_type=F32).astype(BF16)
    kept_rows, kept_cols = gather_kept(kept, block_width, 2)
    update = lax.dot_general(
        kept_rows, kept_cols, (((0,), (0,)), ((), ())), preferred_element_type=F32
    )
    new_covariance = covariance + update * (1.0 / total_tokens)

    def image_part(rows):
        return lax.dot_general(
            new_covariance, rows, (((0,), (0,)), ((), ())), precision=HIGH, preferred_element_type=F32
        )

    image_one, image_rows = reduce_and_spread(image_part(start_rows), 3)
    inverse_one = inverse_factor(total_gram(gram_of(image_one), 4))
    own_rows = lax.dynamic_slice_in_dim(image_rows, f * share_rows, share_rows, 0)
    first_basis = times_transpose(own_rows, inverse_one, root)
    image_two = times_transpose(reduce_over_y(image_part(image_rows), 5), inverse_one)
    total_two, whole_two = total_gram(gram_of(image_two), 6, image_two)
    final_basis = times_transpose(whole_two, inverse_factor(total_two), root)
    return (mlp_out, new_covariance, first_basis, final_basis)


def solution(mesh):
    placed = (
        P("tensor", "fsdp"),
        P("fsdp", "tensor"),
        P("tensor", "fsdp"),
        P("fsdp", None),
        P("fsdp", None),
    )
    return jax.shard_map(
        body,
        mesh=mesh,
        in_specs=placed,
        out_specs=(
            P("fsdp", "tensor"),
            P("tensor", "fsdp"),
            P(("tensor", "fsdp"), None),
            P("fsdp", None),
        ),
        check_vma=False,
    )
```

```python
import functools
import math

import jax
import jax.numpy as jnp
from jax import lax
from jax.experimental import pallas as pl
from jax.experimental.pallas import tpu as pltpu
from jax.sharding import PartitionSpec as P

D = 16384
TOK_DEV = 16
F32 = jnp.float32
BF16 = jnp.bfloat16
HIGH = lax.Precision.HIGH


def inverse_factor_kernel(gram_ref, out_ref, scaled, work, state):
    n = gram_ref.shape[0]
    rows = lax.broadcasted_iota(jnp.int32, (n, n), 0)
    cols = lax.broadcasted_iota(jnp.int32, (n, n), 1)
    gram = gram_ref[...]
    diagonal = jnp.where(rows == cols, gram, 0.0)
    col_scale = lax.rsqrt(jnp.sum(diagonal, axis=1, keepdims=True))
    row_scale = lax.rsqrt(jnp.sum(diagonal, axis=0, keepdims=True))
    scaled[...] = gram * col_scale * row_scale

    def half_lower(residual):
        return jnp.where(rows > cols, residual, jnp.where(rows == cols, 0.5 * residual, 0.0))

    def residual_of(x, precision):
        left = jnp.dot(x, scaled[...], precision=precision, preferred_element_type=F32)
        full = lax.dot_general(
            left, x, (((1,), (1,)), ((), ())), precision=precision, preferred_element_type=F32
        )
        return full - jnp.where(rows == cols, 1.0, 0.0)

    eye = jnp.where(rows == cols, 1.0, 0.0)
    work[...] = eye - half_lower(scaled[...] - eye)

    @pl.loop(0, 2)
    def _(step):
        x = work[...]
        residual = residual_of(x, None)
        work[...] = x - jnp.dot(half_lower(residual), x, preferred_element_type=F32)

    state[0] = 1.0

    def unfinished(step):
        error = state[0]
        return jnp.logical_and(step < 12, jnp.logical_not(error < 1e-3))

    def refine(step):
        x = work[...]
        residual = residual_of(x, HIGH)
        work[...] = x - jnp.dot(half_lower(residual), x, preferred_element_type=F32)
        state[0] = jnp.sum(residual * residual)
        return step + 1

    lax.while_loop(unfinished, refine, 0)

    @pl.when(jnp.logical_not(state[0] < 1e-3))
    def _():
        work[...] = eye

        @pl.loop(0, n)
        def _(j):
            here = cols[0:1] == j
            pivot_row = scaled[pl.ds(j, 1), :]
            pivot = lax.rsqrt(jnp.sum(jnp.where(here, pivot_row, 0.0), axis=1, keepdims=True))
            left = jnp.sum(jnp.where(cols == j, scaled[...], 0.0), axis=1, keepdims=True) * pivot
            left = jnp.where(rows[:, 0:1] > j, left, 0.0)
            own = work[pl.ds(j, 1), :] * pivot
            scaled[...] = scaled[...] - left * (pivot_row * pivot)
            work[...] = work[...] - left * own
            work[pl.ds(j, 1), :] = own

    out_ref[...] = work[...] * row_scale


def inverse_factor(gram):
    n = gram.shape[0]
    return pl.pallas_call(
        inverse_factor_kernel,
        out_shape=jax.ShapeDtypeStruct((n, n), F32),
        in_specs=[pl.BlockSpec(memory_space=pltpu.VMEM)],
        out_specs=pl.BlockSpec(memory_space=pltpu.VMEM),
        scratch_shapes=[pltpu.VMEM((n, n), F32), pltpu.VMEM((n, n), F32), pltpu.SMEM((1,), F32)],
        cost_estimate=pl.CostEstimate(flops=8_000_000_000, bytes_accessed=2 << 20, transcendentals=0),
        name="inverse_factor",
    )(gram)


def times_transpose(rows, factor, scale=1.0):
    out = lax.dot_general(
        rows, factor, (((1,), (1,)), ((), ())), precision=HIGH, preferred_element_type=F32
    )
    return out * scale if scale != 1.0 else out


def gram_of(rows):
    return lax.dot_general(
        rows, rows, (((0,), (0,)), ((), ())), precision=HIGH, preferred_element_type=F32
    )


MESH = pl.DeviceIdType.MESH
RING = 4


class Place:
    def __init__(self):
        f = lax.axis_index("fsdp")
        self.t = lax.axis_index("tensor")
        self.c = lax.rem(f, 2)
        self.x = lax.rem(lax.div(f, 2), RING)
        self.z = lax.div(f, 2 * RING)

    def along(self, axis, step):
        return lax.rem(getattr(self, axis) + (step + RING), RING)

    def device(self, **moved):
        at = {name: moved.get(name, getattr(self, name)) for name in ("z", "x", "c", "t")}
        return {"fsdp": (at["z"] * RING + at["x"]) * 2 + at["c"], "tensor": at["t"]}

    def ahead(self, axis, step):
        return self.device(**{axis: self.along(axis, step)})

    def other_core(self):
        return self.device(c=1 - self.c)


def meet(devices, place=None):
    barrier = pltpu.get_barrier_semaphore()
    for device in devices:
        pl.semaphore_signal(barrier, inc=1, device_id=device, device_id_type=MESH)
    count = len(devices)
    if place is not None:

        @pl.when(place.t != place.z)
        def _():
            pl.semaphore_signal(
                barrier, inc=1, device_id=place.device(z=place.t, t=place.z), device_id_type=MESH
            )

        count = count + jnp.where(place.t != place.z, 1, 0)
    pl.semaphore_wait(barrier, count)


class Links:
    def __init__(self, send, recv):
        self.send, self.recv, self.started = send, recv, []

    def copy(self, src, dst, device):
        i = len(self.started)
        made = pltpu.make_async_remote_copy(
            src_ref=src,
            dst_ref=dst,
            send_sem=self.send.at[i],
            recv_sem=self.recv.at[i],
            device_id=device,
            device_id_type=MESH,
        )
        self.started.append(made)
        return made

    def go(self, src, dst, device):
        made = self.copy(src, dst, device)
        made.start()
        return made


def gather_plane(own, out, slot, width, links, place):
    half, piece = width // 2, width // 4
    ways = ((0, "x", "z"), (1, "z", "x"))

    def at(z, x, cols):
        return out.at[slot(z, x, place.c) + (slice(None), cols)]

    def spot(axis, step, cols):
        z = place.along("z", step) if axis == "z" else place.z
        x = place.along("x", step) if axis == "x" else place.x
        return at(z, x, cols)

    def line(axis, other, step, cols):
        if axis == "x":
            return at(place.along(other, step), slice(None), cols)
        return at(slice(None), place.along(other, step), cols)

    def half_cols(h):
        return pl.ds(h * half, half)

    def piece_cols(h, d):
        return pl.ds(h * half + (0 if d > 0 else piece), piece)

    first, second, third, fourth, rest = {}, {}, {}, {}, []
    for h, axis, _ in ways:
        for d in (1, -1):
            cols = half_cols(h)
            first[h, d] = links.go(own.at[:, cols], spot(axis, 0, cols), place.ahead(axis, d))
    for h, axis, _ in ways:
        for d in (1, -1):
            first[h, d].wait_recv()
            cols = piece_cols(h, d)
            chunk = spot(axis, -d, cols)
            second[h, d] = links.go(chunk, chunk, place.ahead(axis, d))
    return ways, line, half_cols, piece_cols, second, third, fourth, rest


def finish_plane(parts, links, place):
    ways, line, half_cols, piece_cols, second, third, fourth, rest = parts
    for h, axis, other in ways:
        for d in (1, -1):
            second[h, d].wait_recv()
        whole = line(axis, other, 0, half_cols(h))
        for d in (1, -1):
            third[h, d] = links.go(whole, whole, place.ahead(other, d))
        rest.append(links.go(whole, whole, place.other_core()))
    for h, axis, other in ways:
        for d in (1, -1):
            third[h, d].wait_recv()
            part = line(axis, other, -d, piece_cols(h, d))
            fourth[h, d] = links.go(part, part, place.ahead(other, d))
            whole = line(axis, other, -d, half_cols(h))
            rest.append(links.go(whole, whole, place.other_core()))
    for h, axis, other in ways:
        for d in (1, -1):
            fourth[h, d].wait_recv()
            part = line(axis, other, -2 * d, piece_cols(h, d))
            rest.append(links.go(part, part, place.other_core()))
    for made in rest:
        made.wait_recv()


GATHER_COPIES = 26


def plane_neighbours(place):
    return [place.ahead(axis, d) for axis in ("x", "z") for d in (1, -1)] + [place.other_core()]


def by_column(z, x, c):
    return (x, c, z)


def by_token(z, x, c):
    return (z, x, c)


def swap_in(share, out, links, place, sem):
    sent = links.copy(
        share, out.at[by_column(place.t, place.x, place.c)], place.device(z=place.t, t=place.z)
    )

    @pl.when(place.t != place.z)
    def _():
        sent.start()
        sent.wait_recv()

    @pl.when(place.t == place.z)
    def _():
        kept = pltpu.make_async_copy(share, out.at[by_column(place.z, place.x, place.c)], sem)
        kept.start()
        kept.wait()

    return sent


def settle(links, place, swapped):
    for made in links.started:
        if made is swapped:

            @pl.when(place.t != place.z)
            def _():
                made.wait_send()
        else:
            made.wait_send()


CODE_PAD = 16


def encode(share, codes):
    rows = share.shape[0]
    largest = jnp.maximum(jnp.max(jnp.abs(share), axis=0, keepdims=True), 1e-30)
    exponent = jnp.ceil(jnp.log2(largest) - 14.99)
    scaled = jnp.clip(jnp.round(share * jnp.exp2(-exponent)), -32767.0, 32767.0)
    codes[pl.ds(0, rows), :] = scaled.astype(jnp.int32).astype(jnp.int16)
    marks = jnp.broadcast_to(exponent.astype(jnp.int32), (CODE_PAD, share.shape[1]))
    codes[pl.ds(rows, CODE_PAD), :] = marks.astype(jnp.int16)
    return scaled * jnp.exp2(exponent)


def decode(codes):
    wide = codes.astype(jnp.int32).astype(F32)
    rows = codes.shape[0] - CODE_PAD
    return wide[:rows] * jnp.exp2(wide[rows : rows + 1])


def spread_codes(codes, out_ref, links, place, sem):
    swapped = swap_in(codes, out_ref, links, place, sem)
    own = out_ref.at[by_column(place.z, place.x, place.c)]
    parts = gather_plane(own, out_ref, by_column, codes.shape[1], links, place)
    finish_plane(parts, links, place)
    settle(links, place, swapped)


def spread_kernel(share_ref, out_ref, codes, send, recv, sem):
    place = Place()
    links = Links(send, recv)
    meet(plane_neighbours(place), place)
    encode(share_ref[...], codes)
    spread_codes(codes, out_ref, links, place, sem)


def spread_shape(rows, width):
    return jax.ShapeDtypeStruct((RING, 2, RING, rows + CODE_PAD, width), jnp.int16)


def spread(share, collective_id):
    rows, width = share.shape
    return pl.pallas_call(
        spread_kernel,
        out_shape=spread_shape(rows, width),
        in_specs=[pl.BlockSpec(memory_space=pltpu.VMEM)],
        out_specs=pl.BlockSpec(memory_space=pl.ANY),
        scratch_shapes=[
            pltpu.VMEM((rows + CODE_PAD, width), jnp.int16),
            pltpu.SemaphoreType.DMA((GATHER_COPIES + 1,)),
            pltpu.SemaphoreType.DMA((GATHER_COPIES + 1,)),
            pltpu.SemaphoreType.DMA,
        ],
        compiler_params=pltpu.CompilerParams(collective_id=collective_id, has_side_effects=True),
        name="spread",
    )(share)


def reduce_y(part_ref, share_ref, relay, build, arrive, links, place):
    rows, width = share_ref.shape
    half = width // 2
    low, high = pl.ds(0, half), pl.ds(half, half)

    def quarter(step, cols):
        start = pl.multiple_of(place.along("t", step) * rows, rows)
        return part_ref.at[pl.ds(start, rows), cols]

    up, down = place.ahead("t", 1), place.ahead("t", -1)
    far_up = links.go(quarter(2, low), relay.at[0], up)
    far_down = links.go(quarter(2, high), relay.at[1], down)
    near_up = links.go(quarter(1, high), arrive.at[0, :, high], up)
    near_down = links.go(quarter(-1, low), arrive.at[1, :, low], down)
    far_up.wait_recv()
    build[0] = quarter(1, low)[...] + relay[0]
    sum_up = links.go(build.at[0], arrive.at[0, :, low], up)
    far_down.wait_recv()
    build[1] = quarter(-1, high)[...] + relay[1]
    sum_down = links.go(build.at[1], arrive.at[1, :, high], down)
    for made in (near_up, near_down, sum_up, sum_down):
        made.wait_recv()
    share_ref[...] = quarter(0, pl.ds(0, width))[...] + (arrive[0] + arrive[1])


REDUCE_COPIES = 6


def reduce_scratch(rows, width):
    return [
        pltpu.VMEM((2, rows, width // 2), F32),
        pltpu.VMEM((2, rows, width // 2), F32),
        pltpu.VMEM((2, rows, width), F32),
    ]


def y_neighbours(place):
    return [place.ahead("t", 1), place.ahead("t", -1)]


def reduce_kernel(part_ref, share_ref, relay, build, arrive, send, recv):
    place = Place()
    links = Links(send, recv)
    meet(y_neighbours(place))
    reduce_y(part_ref, share_ref, relay, build, arrive, links, place)
    for made in links.started:
        made.wait_send()


def reduce_over_y(part, collective_id):
    rows, width = part.shape[0] // RING, part.shape[1]
    return pl.pallas_call(
        reduce_kernel,
        out_shape=jax.ShapeDtypeStruct((rows, width), F32),
        in_specs=[pl.BlockSpec(memory_space=pltpu.VMEM)],
        out_specs=pl.BlockSpec(memory_space=pltpu.VMEM),
        scratch_shapes=reduce_scratch(rows, width)
        + [pltpu.SemaphoreType.DMA((REDUCE_COPIES,)), pltpu.SemaphoreType.DMA((REDUCE_COPIES,))],
        compiler_params=pltpu.CompilerParams(collective_id=collective_id, has_side_effects=True),
        name="reduce_over_y",
    )(part)


def reduce_spread_kernel(part_ref, share_ref, out_ref, relay, build, arrive, codes, send, recv, sem):
    place = Place()
    links = Links(send, recv)
    meet(plane_neighbours(place) + y_neighbours(place), place)
    reduce_y(part_ref, share_ref, relay, build, arrive, links, place)
    share_ref[...] = encode(share_ref[...], codes)
    spread_codes(codes, out_ref, links, place, sem)


def reduce_and_spread(part, collective_id):
    rows, width = part.shape[0] // RING, part.shape[1]
    copies = REDUCE_COPIES + 1 + GATHER_COPIES
    return pl.pallas_call(
        reduce_spread_kernel,
        out_shape=(jax.ShapeDtypeStruct((rows, width), F32), spread_shape(rows, width)),
        in_specs=[pl.BlockSpec(memory_space=pltpu.VMEM)],
        out_specs=(pl.BlockSpec(memory_space=pltpu.VMEM), pl.BlockSpec(memory_space=pl.ANY)),
        scratch_shapes=reduce_scratch(rows, width)
        + [
            pltpu.VMEM((rows + CODE_PAD, width), jnp.int16),
            pltpu.SemaphoreType.DMA((copies,)),
            pltpu.SemaphoreType.DMA((copies,)),
            pltpu.SemaphoreType.DMA,
        ],
        compiler_params=pltpu.CompilerParams(collective_id=collective_id, has_side_effects=True),
        name="reduce_and_spread",
    )(part)


def image_block(tile, codes_ref, out_ref):
    rows = jnp.concatenate([decode(codes_ref[0, 0, i]) for i in range(RING)], axis=0)
    part = lax.dot_general(
        tile, rows, (((0,), (0,)), ((), ())), precision=HIGH, preferred_element_type=F32
    )

    @pl.when(pl.program_id(0) == 0)
    def _():
        out_ref[...] = part

    @pl.when(pl.program_id(0) > 0)
    def _():
        out_ref[...] += part


def image_kernel(tile_ref, codes_ref, out_ref):
    image_block(tile_ref[...], codes_ref, out_ref)


def update_kernel(scale, tile_ref, codes_ref, kept_rows_ref, kept_cols_ref, new_ref, out_ref):
    update = lax.dot_general(
        kept_rows_ref[...], kept_cols_ref[...], (((0,), (0,)), ((), ())), preferred_element_type=F32
    )
    tile = tile_ref[...] + update * scale
    new_ref[...] = tile
    image_block(tile, codes_ref, out_ref)


def image_part(tile, codes, kept=None, scale=None):
    width = tile.shape[1]
    height = RING * (codes.shape[3] - CODE_PAD)
    tile_spec = pl.BlockSpec((height, width), lambda i: (i, 0))
    code_spec = pl.BlockSpec((1, 1) + codes.shape[2:], lambda i: (i // 2, i % 2, 0, 0, 0))
    out_spec = pl.BlockSpec((width, codes.shape[4]), lambda i: (0, 0))
    out_shape = jax.ShapeDtypeStruct((width, codes.shape[4]), F32)
    if kept is None:
        return pl.pallas_call(
            image_kernel,
            grid=(tile.shape[0] // height,),
            out_shape=out_shape,
            in_specs=[tile_spec, code_spec],
            out_specs=out_spec,
            name="image",
        )(tile, codes)
    kept_rows, kept_cols = kept
    tokens = kept_rows.shape[0]
    return pl.pallas_call(
        functools.partial(update_kernel, scale),
        grid=(tile.shape[0] // height,),
        out_shape=(jax.ShapeDtypeStruct(tile.shape, F32), out_shape),
        in_specs=[
            tile_spec,
            code_spec,
            pl.BlockSpec((tokens, height), lambda i: (0, i)),
            pl.BlockSpec(kept_cols.shape, lambda i: (0, 0)),
        ],
        out_specs=(tile_spec, out_spec),
        name="update_image",
    )(tile, codes, kept_rows, kept_cols)


def mlp_kernel(
    hidden_ref, weight_ref, out_ref, hid, weight, part, pair, far1, near1, far2, near2, send, recv, sem
):
    place = Place()
    links = Links(send, recv)
    load = pltpu.make_async_copy(weight_ref, weight, sem)
    load.start()
    meet(plane_neighbours(place) + y_neighbours(place))
    tokens = hidden_ref.shape[0]
    width = weight.shape[1]
    half, piece, tile = width // 2, width // 4, 512
    up, down = place.ahead("t", 1), place.ahead("t", -1)
    c = place.c
    to_up = links.go(hidden_ref, hid.at[place.t], up)
    to_down = links.go(hidden_ref, hid.at[place.t], down)
    load.wait()

    def product(group, rows):
        @pl.loop(0, width // tile)
        def _(j):
            cols = pl.ds(pl.multiple_of(j * tile, tile), tile)
            block = jnp.dot(rows[...], weight[:, cols], preferred_element_type=F32)
            part[group, :, :, :, cols] = block.reshape(RING, 2, tokens // (2 * RING), tile)

        return links.go(part.at[group, :, 1 - c], pair.at[group], place.other_core())

    pairs = [product(place.t, hidden_ref)]
    below, above, across = place.along("t", -1), place.along("t", 1), place.along("t", 2)
    to_up.wait_recv()
    first = hid.at[below, pl.ds(0, tokens // 2)]
    on_up = links.go(first, first, up)
    to_down.wait_recv()
    second = hid.at[above, pl.ds(tokens // 2, tokens // 2)]
    on_down = links.go(second, second, down)
    pairs.append(product(below, hid.at[below]))
    pairs.append(product(above, hid.at[above]))
    on_up.wait_recv()
    on_down.wait_recv()
    pairs.append(product(across, hid.at[across]))
    for group, made in zip((place.t, below, above, across), pairs):
        made.wait_recv()

        @pl.loop(0, RING)
        def _(i):
            part[group, i, c] = part[group, i, c] + pair[group, i]

    ways = ((0, "z", "x"), (1, "x", "z"))

    def half_cols(h):
        return pl.ds(h * half, half)

    def piece_cols(h, d):
        return pl.ds(h * half + (0 if d > 0 else piece), piece)

    def in_half(d):
        return pl.ds(0 if d > 0 else piece, piece)

    def line(axis, step, cols, i=slice(None)):
        if axis == "z":
            return part.at[place.along("z", step), i, c, :, cols]
        return part.at[i, place.along("x", step), c, :, cols]

    def block(other, step, cols):
        if other == "z":
            return part.at[place.along("z", step), place.x, c, :, cols]
        return part.at[place.z, place.along("x", step), c, :, cols]

    def add(into, value):
        into[...] = into[...] + value

    far, early, late = {}, {}, {}
    for h, axis, _ in ways:
        for n, d in enumerate((1, -1)):
            far[h, d] = links.go(line(axis, 2, piece_cols(h, d)), far1.at[h, n], place.ahead(axis, d))
    for h, axis, _ in ways:
        for n, d in enumerate((1, -1)):
            early[h, d] = links.go(
                line(axis, d, piece_cols(h, -d)), near1.at[h, n, :, :, in_half(-d)], place.ahead(axis, d)
            )
    for h, axis, _ in ways:
        for n, d in enumerate((1, -1)):
            far[h, d].wait_recv()

            @pl.loop(0, RING)
            def _(i):
                add(line(axis, d, piece_cols(h, d), i), far1[h, n, i])

            late[h, d] = links.go(
                line(axis, d, piece_cols(h, d)), near1.at[h, n, :, :, in_half(d)], place.ahead(axis, d)
            )
    for h, axis, other in ways:
        for d in (1, -1):
            early[h, d].wait_recv()
            late[h, d].wait_recv()

        @pl.loop(0, RING)
        def _(i):
            add(line(axis, 0, half_cols(h), i), near1[h, 0, i] + near1[h, 1, i])

        for n, d in enumerate((1, -1)):
            far[h, d] = links.go(block(other, 2, piece_cols(h, d)), far2.at[h, n], place.ahead(other, d))
        for n, d in enumerate((1, -1)):
            early[h, d] = links.go(
                block(other, d, piece_cols(h, -d)), near2.at[h, n, :, in_half(-d)], place.ahead(other, d)
            )
    for h, axis, other in ways:
        for n, d in enumerate((1, -1)):
            far[h, d].wait_recv()
            add(block(other, d, piece_cols(h, d)), far2[h, n])
            late[h, d] = links.go(
                block(other, d, piece_cols(h, d)), near2.at[h, n, :, in_half(d)], place.ahead(other, d)
            )
    for h, axis, other in ways:
        for d in (1, -1):
            early[h, d].wait_recv()
            late[h, d].wait_recv()
        total = block(other, 0, half_cols(h))[...] + (near2[h, 0] + near2[h, 1])
        out_ref[:, half_cols(h)] = total.astype(out_ref.dtype)
    for made in links.started:
        made.wait_send()


def down_projection(hidden, weight, collective_id):
    tokens, depth = hidden.shape
    width = weight.shape[1]
    rows = tokens // (2 * RING)
    copies = 32
    return pl.pallas_call(
        mlp_kernel,
        out_shape=jax.ShapeDtypeStruct((rows, width), BF16),
        in_specs=[pl.BlockSpec(memory_space=pltpu.VMEM), pl.BlockSpec(memory_space=pl.ANY)],
        out_specs=pl.BlockSpec(memory_space=pltpu.VMEM),
        scratch_shapes=[
            pltpu.VMEM((RING, tokens, depth), BF16),
            pltpu.VMEM((depth, width), BF16),
            pltpu.VMEM((RING, RING, 2, rows, width), F32),
            pltpu.VMEM((RING, RING, rows, width), F32),
            pltpu.VMEM((2, 2, RING, rows, width // 4), F32),
            pltpu.VMEM((2, 2, RING, rows, width // 2), F32),
            pltpu.VMEM((2, 2, rows, width // 4), F32),
            pltpu.VMEM((2, 2, rows, width // 2), F32),
            pltpu.SemaphoreType.DMA((copies,)),
            pltpu.SemaphoreType.DMA((copies,)),
            pltpu.SemaphoreType.DMA,
        ],
        compiler_params=pltpu.CompilerParams(collective_id=collective_id, has_side_effects=True),
        name="down_projection",
    )(hidden, weight)


def kept_kernel(kept_ref, rows_ref, cols_ref, send, recv, sem):
    place = Place()
    links = Links(send, recv)
    meet(plane_neighbours(place) + y_neighbours(place))
    local = pltpu.make_async_copy(kept_ref, rows_ref.at[by_token(place.z, place.x, place.c)], sem)
    local.start()
    parts = gather_plane(kept_ref, rows_ref, by_token, kept_ref.shape[1], links, place)
    local.wait()
    finish_plane(parts, links, place)
    for made in links.started:
        made.wait_send()
    width = cols_ref.shape[-1]
    start = pl.multiple_of((place.x * 2 + place.c) * width, width)
    source = rows_ref.at[:, :, :, :, pl.ds(start, width)]
    distance = lax.rem(place.t - place.z + RING, RING)
    up, down = place.ahead("t", 1), place.ahead("t", -1)
    to_up = links.copy(source, cols_ref, up)
    to_down = links.copy(source, cols_ref, down)
    low = cols_ref.at[pl.ds(0, RING // 2)]
    high = cols_ref.at[pl.ds(RING // 2, RING // 2)]
    on_up = links.copy(low, low, up)
    on_down = links.copy(high, high, down)

    @pl.when(distance == 0)
    def _():
        to_up.start()
        to_down.start()
        own = pltpu.make_async_copy(source, cols_ref, sem)
        own.start()
        own.wait()
        to_up.wait_send()
        to_down.wait_send()

    @pl.when(distance == 1)
    def _():
        to_up.wait_recv()
        on_up.start()
        on_up.wait_send()

    @pl.when(distance == 3)
    def _():
        to_down.wait_recv()
        on_down.start()
        on_down.wait_send()

    @pl.when(distance == 2)
    def _():
        on_up.wait_recv()
        on_down.wait_recv()


def gather_kept(kept, tile_width, collective_id):
    rows, width = kept.shape
    lead = (RING, RING, 2, rows)
    copies = GATHER_COPIES + 4
    kept_rows, kept_cols = pl.pallas_call(
        kept_kernel,
        out_shape=(
            jax.ShapeDtypeStruct(lead + (width,), kept.dtype),
            jax.ShapeDtypeStruct(lead + (tile_width,), kept.dtype),
        ),
        in_specs=[pl.BlockSpec(memory_space=pltpu.VMEM)],
        out_specs=(pl.BlockSpec(memory_space=pltpu.VMEM), pl.BlockSpec(memory_space=pltpu.VMEM)),
        scratch_shapes=[
            pltpu.SemaphoreType.DMA((copies,)),
            pltpu.SemaphoreType.DMA((copies,)),
            pltpu.SemaphoreType.DMA,
        ],
        compiler_params=pltpu.CompilerParams(collective_id=collective_id, has_side_effects=True),
        name="gather_kept",
    )(kept)
    return kept_rows.reshape(-1, width), kept_cols.reshape(-1, tile_width)


def total_kernel(with_rows, *refs):
    if with_rows:
        gram_ref, rows_ref, out_ref, all_ref = refs[:4]
        refs = refs[4:]
    else:
        gram_ref, out_ref = refs[:2]
        refs = refs[2:]
    pair, mine, first, second, last, sum_one, sum_two, send, recv = refs
    place = Place()
    links = Links(send, recv)
    n = gram_ref.shape[0]
    half, width = n // 2, n // 2
    block, piece = half // RING, half // RING // RING
    ways = (("x", "z", pl.ds(0, width)), ("z", "x", pl.ds(width, width)))
    meet(
        [place.other_core()]
        + [place.ahead(axis, k) for axis in ("x", "z", "t") for k in (1, 2, 3)]
    )
    kept_base = pl.multiple_of(place.c * half, half)
    gone_base = pl.multiple_of((1 - place.c) * half, half)
    swapped = links.go(gram_ref.at[pl.ds(gone_base, half)], pair, place.other_core())
    relayed = []
    if with_rows:
        around = all_ref.at[place.t]
        relayed = [links.go(rows_ref, around, place.ahead("t", d)) for d in (1, -1)]
        all_ref[pl.ds(place.t, 1)] = rows_ref[...][None]
    swapped.wait_recv()
    mine[...] = gram_ref[pl.ds(kept_base, half), :] + pair[...]
    sent = {}
    for p, (axis, other, cols) in enumerate(ways):
        for k in (1, 2, 3):
            start = pl.multiple_of(place.along(axis, k) * block, block)
            sent[p, k] = links.go(
                mine.at[pl.ds(start, block), cols], first.at[p, k - 1], place.ahead(axis, k)
            )
    for p, (axis, other, cols) in enumerate(ways):
        for k in (1, 2, 3):
            sent[p, k].wait_recv()
        start = pl.multiple_of(getattr(place, axis) * block, block)
        sum_one[p] = (mine[pl.ds(start, block), cols] + first[p, 0]) + (first[p, 1] + first[p, 2])
        for k in (1, 2, 3):
            start = pl.multiple_of(place.along(other, k) * piece, piece)
            sent[p, k] = links.go(
                sum_one.at[p, pl.ds(start, piece)], second.at[p, k - 1], place.ahead(other, k)
            )
    for p, (axis, other, cols) in enumerate(ways):
        for k in (1, 2, 3):
            sent[p, k].wait_recv()
        start = pl.multiple_of(getattr(place, other) * piece, piece)
        sum_two[p] = (sum_one[p, pl.ds(start, piece), :] + second[p, 0]) + (second[p, 1] + second[p, 2])
        for k in (1, 2, 3):
            sent[p, k] = links.go(sum_two.at[p], last.at[p, place.t], place.ahead("t", k))
        last[p, pl.ds(place.t, 1)] = sum_two[p][None]
    for p, (axis, other, cols) in enumerate(ways):
        for k in (1, 2, 3):
            sent[p, k].wait_recv()
        base = kept_base + getattr(place, axis) * block
        start = pl.multiple_of(base + getattr(place, other) * piece, piece)
        final = out_ref.at[pl.ds(start, piece), cols]
        final[...] = (last[p, 0] + last[p, 1]) + (last[p, 2] + last[p, 3])
        for k in (1, 2, 3):
            sent[p, k] = links.go(final, final, place.ahead(other, k))
    if with_rows:
        part = rows_ref.shape[0] // 2
        onward = []
        for d, made in zip((1, -1), relayed):
            made.wait_recv()
            held = all_ref.at[place.along("t", -d), pl.ds(0 if d > 0 else part, part)]
            onward.append(links.go(held, held, place.ahead("t", d)))
    for p, (axis, other, cols) in enumerate(ways):
        for k in (1, 2, 3):
            sent[p, k].wait_recv()
        start = pl.multiple_of(kept_base + getattr(place, axis) * block, block)
        whole = out_ref.at[pl.ds(start, block), cols]
        for k in (1, 2, 3):
            sent[p, k] = links.go(whole, whole, place.ahead(axis, k))
    for p in range(2):
        for k in (1, 2, 3):
            sent[p, k].wait_recv()
    side = out_ref.at[pl.ds(kept_base, half)]
    links.go(side, side, place.other_core()).wait_recv()
    if with_rows:
        for made in onward:
            made.wait_recv()
    for made in links.started:
        made.wait_send()


def total_gram(gram, collective_id, rows=None):
    n = gram.shape[0]
    block, piece = n // 2 // RING, n // 2 // RING // RING
    copies = 2 + 30 + (4 if rows is not None else 0)
    shapes = [jax.ShapeDtypeStruct((n, n), F32)]
    operands = [gram]
    if rows is not None:
        shapes.append(jax.ShapeDtypeStruct((RING,) + rows.shape, F32))
        operands.append(rows)
    vmem = pl.BlockSpec(memory_space=pltpu.VMEM)
    out = pl.pallas_call(
        functools.partial(total_kernel, rows is not None),
        out_shape=tuple(shapes),
        in_specs=[vmem] * len(operands),
        out_specs=tuple([vmem] * len(shapes)),
        scratch_shapes=[
            pltpu.VMEM((n // 2, n), F32),
            pltpu.VMEM((n // 2, n), F32),
            pltpu.VMEM((2, 3, block, n // 2), F32),
            pltpu.VMEM((2, 3, piece, n // 2), F32),
            pltpu.VMEM((2, RING, piece, n // 2), F32),
            pltpu.VMEM((2, block, n // 2), F32),
            pltpu.VMEM((2, piece, n // 2), F32),
            pltpu.SemaphoreType.DMA((copies,)),
            pltpu.SemaphoreType.DMA((copies,)),
        ],
        compiler_params=pltpu.CompilerParams(collective_id=collective_id, has_side_effects=True),
        name="total_gram",
    )(*operands)
    if rows is None:
        return out[0]
    return out[0], out[1].reshape(-1, rows.shape[1])


def body(hidden, down_weight, covariance, keep_index, start_basis):
    fsdp_count = lax.axis_size("fsdp")
    total_tokens = TOK_DEV * fsdp_count
    quarter, block_width = covariance.shape
    share_rows = quarter // fsdp_count
    f = lax.axis_index("fsdp")
    t = lax.axis_index("tensor")
    root = math.sqrt(D)

    start_share = lax.dynamic_slice_in_dim(start_basis, t * share_rows, share_rows, 0)
    start_codes = spread(start_share, 1)

    mlp_out = down_projection(hidden, down_weight, 0)
    listed = keep_index[0]
    positions = jnp.arange(mlp_out.shape[0], dtype=jnp.int32)
    chosen = (listed[:, None] == positions[None, :]).astype(BF16)
    kept = jnp.dot(chosen, mlp_out, preferred_element_type=F32).astype(BF16)
    kept_pair = gather_kept(kept, block_width, 2)
    new_covariance, part_one = image_part(covariance, start_codes, kept_pair, 1.0 / total_tokens)
    image_one, codes_one = reduce_and_spread(part_one, 3)
    inverse_one = inverse_factor(total_gram(gram_of(image_one), 4))
    every = codes_one.reshape(fsdp_count, -1, codes_one.shape[-1])
    own_rows = decode(lax.dynamic_index_in_dim(every, f, 0, keepdims=False))
    first_basis = times_transpose(own_rows, inverse_one, root)
    image_two = times_transpose(reduce_over_y(image_part(new_covariance, codes_one), 5), inverse_one)
    total_two, whole_two = total_gram(gram_of(image_two), 6, image_two)
    final_basis = times_transpose(whole_two, inverse_factor(total_two), root)
    return (mlp_out, new_covariance, first_basis, final_basis)


def solution(mesh):
    placed = (
        P("tensor", "fsdp"),
        P("fsdp", "tensor"),
        P("tensor", "fsdp"),
        P("fsdp", None),
        P("fsdp", None),
    )
    return jax.shard_map(
        body,
        mesh=mesh,
        in_specs=placed,
        out_specs=(
            P("fsdp", "tensor"),
            P("tensor", "fsdp"),
            P(("tensor", "fsdp"), None),
            P("fsdp", None),
        ),
        check_vma=False,
    )
```

```python
import functools
import math

import jax
import jax.numpy as jnp
from jax import lax
from jax.experimental import pallas as pl
from jax.experimental.pallas import tpu as pltpu
from jax.sharding import PartitionSpec as P

D = 16384
TOK_DEV = 16
F32 = jnp.float32
BF16 = jnp.bfloat16
HIGH = lax.Precision.HIGH


def inverse_factor_kernel(gram_ref, out_ref, scaled, work, state):
    n = gram_ref.shape[0]
    rows = lax.broadcasted_iota(jnp.int32, (n, n), 0)
    cols = lax.broadcasted_iota(jnp.int32, (n, n), 1)
    gram = gram_ref[...]
    diagonal = jnp.where(rows == cols, gram, 0.0)
    col_scale = lax.rsqrt(jnp.sum(diagonal, axis=1, keepdims=True))
    row_scale = lax.rsqrt(jnp.sum(diagonal, axis=0, keepdims=True))
    scaled[...] = gram * col_scale * row_scale

    def half_lower(residual):
        return jnp.where(rows > cols, residual, jnp.where(rows == cols, 0.5 * residual, 0.0))

    def residual_of(x, precision):
        left = jnp.dot(x, scaled[...], precision=precision, preferred_element_type=F32)
        full = lax.dot_general(
            left, x, (((1,), (1,)), ((), ())), precision=precision, preferred_element_type=F32
        )
        return full - jnp.where(rows == cols, 1.0, 0.0)

    eye = jnp.where(rows == cols, 1.0, 0.0)
    work[...] = eye - half_lower(scaled[...] - eye)

    @pl.loop(0, 2)
    def _(step):
        x = work[...]
        residual = residual_of(x, None)
        work[...] = x - jnp.dot(half_lower(residual), x, preferred_element_type=F32)

    state[0] = 1.0

    def unfinished(step):
        error = state[0]
        return jnp.logical_and(step < 12, jnp.logical_not(error < 1e-3))

    def refine(step):
        x = work[...]
        residual = residual_of(x, HIGH)
        work[...] = x - jnp.dot(half_lower(residual), x, preferred_element_type=F32)
        state[0] = jnp.sum(residual * residual)
        return step + 1

    lax.while_loop(unfinished, refine, 0)

    @pl.when(jnp.logical_not(state[0] < 1e-3))
    def _():
        work[...] = eye

        @pl.loop(0, n)
        def _(j):
            here = cols[0:1] == j
            pivot_row = scaled[pl.ds(j, 1), :]
            pivot = lax.rsqrt(jnp.sum(jnp.where(here, pivot_row, 0.0), axis=1, keepdims=True))
            left = jnp.sum(jnp.where(cols == j, scaled[...], 0.0), axis=1, keepdims=True) * pivot
            left = jnp.where(rows[:, 0:1] > j, left, 0.0)
            own = work[pl.ds(j, 1), :] * pivot
            scaled[...] = scaled[...] - left * (pivot_row * pivot)
            work[...] = work[...] - left * own
            work[pl.ds(j, 1), :] = own

    out_ref[...] = work[...] * row_scale


def inverse_factor(gram):
    n = gram.shape[0]
    return pl.pallas_call(
        inverse_factor_kernel,
        out_shape=jax.ShapeDtypeStruct((n, n), F32),
        in_specs=[pl.BlockSpec(memory_space=pltpu.VMEM)],
        out_specs=pl.BlockSpec(memory_space=pltpu.VMEM),
        scratch_shapes=[pltpu.VMEM((n, n), F32), pltpu.VMEM((n, n), F32), pltpu.SMEM((1,), F32)],
        cost_estimate=pl.CostEstimate(flops=8_000_000_000, bytes_accessed=2 << 20, transcendentals=0),
        name="inverse_factor",
    )(gram)


def times_transpose(rows, factor, scale=1.0):
    out = lax.dot_general(
        rows, factor, (((1,), (1,)), ((), ())), precision=HIGH, preferred_element_type=F32
    )
    return out * scale if scale != 1.0 else out


MESH = pl.DeviceIdType.MESH
RING = 4


class Place:
    def __init__(self):
        f = lax.axis_index("fsdp")
        self.t = lax.axis_index("tensor")
        self.c = lax.rem(f, 2)
        self.x = lax.rem(lax.div(f, 2), RING)
        self.z = lax.div(f, 2 * RING)

    def along(self, axis, step):
        return lax.rem(getattr(self, axis) + (step + RING), RING)

    def device(self, **moved):
        at = {name: moved.get(name, getattr(self, name)) for name in ("z", "x", "c", "t")}
        return {"fsdp": (at["z"] * RING + at["x"]) * 2 + at["c"], "tensor": at["t"]}

    def ahead(self, axis, step):
        return self.device(**{axis: self.along(axis, step)})

    def other_core(self):
        return self.device(c=1 - self.c)


def meet(devices, place=None):
    barrier = pltpu.get_barrier_semaphore()
    for device in devices:
        pl.semaphore_signal(barrier, inc=1, device_id=device, device_id_type=MESH)
    count = len(devices)
    if place is not None:

        @pl.when(place.t != place.z)
        def _():
            pl.semaphore_signal(
                barrier, inc=1, device_id=place.device(z=place.t, t=place.z), device_id_type=MESH
            )

        count = count + jnp.where(place.t != place.z, 1, 0)
    pl.semaphore_wait(barrier, count)


class Links:
    def __init__(self, send, recv):
        self.send, self.recv, self.started = send, recv, []

    def copy(self, src, dst, device):
        i = len(self.started)
        made = pltpu.make_async_remote_copy(
            src_ref=src,
            dst_ref=dst,
            send_sem=self.send.at[i],
            recv_sem=self.recv.at[i],
            device_id=device,
            device_id_type=MESH,
        )
        self.started.append(made)
        return made

    def go(self, src, dst, device):
        made = self.copy(src, dst, device)
        made.start()
        return made


def gather_steps(own, out, slot, width, links, place):
    half, piece = width // 2, width // 4
    ways = ((0, "x", "z"), (1, "z", "x"))

    def at(z, x, cols):
        return out.at[slot(z, x, place.c) + (slice(None), cols)]

    def spot(axis, step, cols):
        z = place.along("z", step) if axis == "z" else place.z
        x = place.along("x", step) if axis == "x" else place.x
        return at(z, x, cols)

    def line(axis, other, step, cols):
        if axis == "x":
            return at(place.along(other, step), slice(None), cols)
        return at(slice(None), place.along(other, step), cols)

    def half_cols(h):
        return pl.ds(h * half, half)

    def piece_cols(h, d):
        return pl.ds(h * half + (0 if d > 0 else piece), piece)

    made, rest = {}, []
    for h, axis, _ in ways:
        for d in (1, -1):
            cols = half_cols(h)
            made[h, d] = links.go(own.at[:, cols], spot(axis, 0, cols), place.ahead(axis, d))
    yield
    onward = {}
    for h, axis, _ in ways:
        for d in (1, -1):
            made[h, d].wait_recv()
            chunk = spot(axis, -d, piece_cols(h, d))
            onward[h, d] = links.go(chunk, chunk, place.ahead(axis, d))
    yield
    for h, axis, other in ways:
        for d in (1, -1):
            onward[h, d].wait_recv()
        whole = line(axis, other, 0, half_cols(h))
        for d in (1, -1):
            made[h, d] = links.go(whole, whole, place.ahead(other, d))
        rest.append(links.go(whole, whole, place.other_core()))
    yield
    for h, axis, other in ways:
        for d in (1, -1):
            made[h, d].wait_recv()
            part = line(axis, other, -d, piece_cols(h, d))
            onward[h, d] = links.go(part, part, place.ahead(other, d))
            whole = line(axis, other, -d, half_cols(h))
            rest.append(links.go(whole, whole, place.other_core()))
    yield
    for h, axis, other in ways:
        for d in (1, -1):
            onward[h, d].wait_recv()
            part = line(axis, other, -2 * d, piece_cols(h, d))
            rest.append(links.go(part, part, place.other_core()))
    yield
    for made_last in rest:
        made_last.wait_recv()


def run(steps):
    for _ in steps:
        pass


GATHER_COPIES = 26


def plane_neighbours(place):
    return [place.ahead(axis, d) for axis in ("x", "z") for d in (1, -1)] + [place.other_core()]


def by_column(z, x, c):
    return (x, c, z)


def by_token(z, x, c):
    return (z, x, c)


def swap_start(share, out, links, place, sem):
    sent = links.copy(
        share, out.at[by_column(place.t, place.x, place.c)], place.device(z=place.t, t=place.z)
    )
    kept = pltpu.make_async_copy(share, out.at[by_column(place.z, place.x, place.c)], sem)

    @pl.when(place.t != place.z)
    def _():
        sent.start()

    @pl.when(place.t == place.z)
    def _():
        kept.start()

    return sent, kept


def swap_end(swap, place):
    sent, kept = swap

    @pl.when(place.t != place.z)
    def _():
        sent.wait_recv()

    @pl.when(place.t == place.z)
    def _():
        kept.wait()


def settle(links, place, swap=None):
    for made in links.started:
        if swap is not None and made is swap[0]:

            @pl.when(place.t != place.z)
            def _():
                made.wait_send()
        else:
            made.wait_send()


CODE_PAD = 16


def encode(share, codes):
    rows = share.shape[0]
    largest = jnp.maximum(jnp.max(jnp.abs(share), axis=0, keepdims=True), 1e-30)
    exponent = jnp.ceil(jnp.log2(largest) - 14.99)
    scaled = jnp.clip(jnp.round(share * jnp.exp2(-exponent)), -32767.0, 32767.0)
    codes[pl.ds(0, rows), :] = scaled.astype(jnp.int32).astype(jnp.int16)
    marks = jnp.broadcast_to(exponent.astype(jnp.int32), (CODE_PAD, share.shape[1]))
    codes[pl.ds(rows, CODE_PAD), :] = marks.astype(jnp.int16)
    return scaled * jnp.exp2(exponent)


def decode(codes):
    wide = codes.astype(jnp.int32).astype(F32)
    rows = codes.shape[0] - CODE_PAD
    return wide[:rows] * jnp.exp2(wide[rows : rows + 1])


def spread_shape(rows, width):
    return jax.ShapeDtypeStruct((RING, 2, RING, rows + CODE_PAD, width), jnp.int16)


def spread_steps(codes, out_ref, links, place):
    own = out_ref.at[by_column(place.z, place.x, place.c)]
    return gather_steps(own, out_ref, by_column, codes.shape[1], links, place)


def reduce_y(part_ref, share_ref, relay, build, arrive, links, place):
    rows, width = share_ref.shape
    half = width // 2
    low, high = pl.ds(0, half), pl.ds(half, half)

    def quarter(step, cols):
        start = pl.multiple_of(place.along("t", step) * rows, rows)
        return part_ref.at[pl.ds(start, rows), cols]

    up, down = place.ahead("t", 1), place.ahead("t", -1)
    far_up = links.go(quarter(2, low), relay.at[0], up)
    far_down = links.go(quarter(2, high), relay.at[1], down)
    near_up = links.go(quarter(1, high), arrive.at[0, :, high], up)
    near_down = links.go(quarter(-1, low), arrive.at[1, :, low], down)
    far_up.wait_recv()
    build[0] = quarter(1, low)[...] + relay[0]
    sum_up = links.go(build.at[0], arrive.at[0, :, low], up)
    far_down.wait_recv()
    build[1] = quarter(-1, high)[...] + relay[1]
    sum_down = links.go(build.at[1], arrive.at[1, :, high], down)
    for made in (near_up, near_down, sum_up, sum_down):
        made.wait_recv()
    share_ref[...] = quarter(0, pl.ds(0, width))[...] + (arrive[0] + arrive[1])


REDUCE_COPIES = 6


def reduce_scratch(rows, width):
    return [
        pltpu.VMEM((2, rows, width // 2), F32),
        pltpu.VMEM((2, rows, width // 2), F32),
        pltpu.VMEM((2, rows, width), F32),
    ]


def y_neighbours(place):
    return [place.ahead("t", 1), place.ahead("t", -1)]


def image_block(tile, codes_ref, out_ref):
    rows = jnp.concatenate([decode(codes_ref[0, 0, i]) for i in range(RING)], axis=0)
    part = lax.dot_general(
        tile, rows, (((0,), (0,)), ((), ())), precision=HIGH, preferred_element_type=F32
    )

    @pl.when(pl.program_id(0) == 0)
    def _():
        out_ref[...] = part

    @pl.when(pl.program_id(0) > 0)
    def _():
        out_ref[...] += part


def image_kernel(tile_ref, codes_ref, out_ref):
    image_block(tile_ref[...], codes_ref, out_ref)


def update_kernel(scale, tile_ref, codes_ref, kept_rows_ref, kept_cols_ref, new_ref, out_ref):
    update = lax.dot_general(
        kept_rows_ref[...], kept_cols_ref[...], (((0,), (0,)), ((), ())), preferred_element_type=F32
    )
    tile = tile_ref[...] + update * scale
    new_ref[...] = tile
    image_block(tile, codes_ref, out_ref)


def image_part(tile, codes, kept=None, scale=None):
    width = tile.shape[1]
    height = RING * (codes.shape[3] - CODE_PAD)
    tile_spec = pl.BlockSpec((height, width), lambda i: (i, 0))
    code_spec = pl.BlockSpec((1, 1) + codes.shape[2:], lambda i: (i // 2, i % 2, 0, 0, 0))
    out_spec = pl.BlockSpec((width, codes.shape[4]), lambda i: (0, 0))
    out_shape = jax.ShapeDtypeStruct((width, codes.shape[4]), F32)
    if kept is None:
        return pl.pallas_call(
            image_kernel,
            grid=(tile.shape[0] // height,),
            out_shape=out_shape,
            in_specs=[tile_spec, code_spec],
            out_specs=out_spec,
            name="image",
        )(tile, codes)
    kept_rows, kept_cols = kept
    tokens = kept_rows.shape[0]
    return pl.pallas_call(
        functools.partial(update_kernel, scale),
        grid=(tile.shape[0] // height,),
        out_shape=(jax.ShapeDtypeStruct(tile.shape, F32), out_shape),
        in_specs=[
            tile_spec,
            code_spec,
            pl.BlockSpec((tokens, height), lambda i: (0, i)),
            pl.BlockSpec(kept_cols.shape, lambda i: (0, 0)),
        ],
        out_specs=(tile_spec, out_spec),
        name="update_image",
    )(tile, codes, kept_rows, kept_cols)


def mlp_kernel(
    hidden_ref,
    weight_ref,
    start_ref,
    out_ref,
    spread_ref,
    hid,
    weight,
    part,
    pair,
    far1,
    near1,
    far2,
    near2,
    codes,
    send,
    recv,
    sem,
    swap_sem,
):
    place = Place()
    links = Links(send, recv)
    load = pltpu.make_async_copy(weight_ref, weight, sem)
    load.start()
    share_rows = codes.shape[0] - CODE_PAD
    share_start = pl.multiple_of(place.t * share_rows, share_rows)
    encode(start_ref[pl.ds(share_start, share_rows), :], codes)
    meet(plane_neighbours(place) + y_neighbours(place), place)
    tokens = hidden_ref.shape[0]
    width = weight.shape[1]
    half, piece, tile = width // 2, width // 4, 512
    up, down = place.ahead("t", 1), place.ahead("t", -1)
    c = place.c
    to_up = links.go(hidden_ref, hid.at[place.t], up)
    to_down = links.go(hidden_ref, hid.at[place.t], down)
    swap = swap_start(codes, spread_ref, links, place, swap_sem)
    load.wait()

    def product(group, rows):
        @pl.loop(0, width // tile)
        def _(j):
            cols = pl.ds(pl.multiple_of(j * tile, tile), tile)
            block = jnp.dot(rows[...], weight[:, cols], preferred_element_type=F32)
            part[group, :, :, :, cols] = block.reshape(RING, 2, tokens // (2 * RING), tile)

        return links.go(part.at[group, :, 1 - c], pair.at[group], place.other_core())

    pairs = [product(place.t, hidden_ref)]
    swap_end(swap, place)
    spread = spread_steps(codes, spread_ref, links, place)
    next(spread)
    below, above, across = place.along("t", -1), place.along("t", 1), place.along("t", 2)
    to_up.wait_recv()
    first = hid.at[below, pl.ds(0, tokens // 2)]
    on_up = links.go(first, first, up)
    to_down.wait_recv()
    second = hid.at[above, pl.ds(tokens // 2, tokens // 2)]
    on_down = links.go(second, second, down)
    next(spread)
    pairs.append(product(below, hid.at[below]))
    next(spread)
    pairs.append(product(above, hid.at[above]))
    on_up.wait_recv()
    on_down.wait_recv()
    pairs.append(product(across, hid.at[across]))
    next(spread)
    for group, made in zip((place.t, below, above, across), pairs):
        made.wait_recv()

        @pl.loop(0, RING)
        def _(i):
            part[group, i, c] = part[group, i, c] + pair[group, i]

    next(spread)
    ways = ((0, "z", "x"), (1, "x", "z"))

    def half_cols(h):
        return pl.ds(h * half, half)

    def piece_cols(h, d):
        return pl.ds(h * half + (0 if d > 0 else piece), piece)

    def in_half(d):
        return pl.ds(0 if d > 0 else piece, piece)

    def line(axis, step, cols, i=slice(None)):
        if axis == "z":
            return part.at[place.along("z", step), i, c, :, cols]
        return part.at[i, place.along("x", step), c, :, cols]

    def block(other, step, cols):
        if other == "z":
            return part.at[place.along("z", step), place.x, c, :, cols]
        return part.at[place.z, place.along("x", step), c, :, cols]

    def add(into, value):
        into[...] = into[...] + value

    far, early, late = {}, {}, {}
    for h, axis, _ in ways:
        for n, d in enumerate((1, -1)):
            far[h, d] = links.go(line(axis, 2, piece_cols(h, d)), far1.at[h, n], place.ahead(axis, d))
    for h, axis, _ in ways:
        for n, d in enumerate((1, -1)):
            early[h, d] = links.go(
                line(axis, d, piece_cols(h, -d)), near1.at[h, n, :, :, in_half(-d)], place.ahead(axis, d)
            )
    for h, axis, _ in ways:
        for n, d in enumerate((1, -1)):
            far[h, d].wait_recv()

            @pl.loop(0, RING)
            def _(i):
                add(line(axis, d, piece_cols(h, d), i), far1[h, n, i])

            late[h, d] = links.go(
                line(axis, d, piece_cols(h, d)), near1.at[h, n, :, :, in_half(d)], place.ahead(axis, d)
            )
    for h, axis, other in ways:
        for d in (1, -1):
            early[h, d].wait_recv()
            late[h, d].wait_recv()

        @pl.loop(0, RING)
        def _(i):
            add(line(axis, 0, half_cols(h), i), near1[h, 0, i] + near1[h, 1, i])

        for n, d in enumerate((1, -1)):
            far[h, d] = links.go(block(other, 2, piece_cols(h, d)), far2.at[h, n], place.ahead(other, d))
        for n, d in enumerate((1, -1)):
            early[h, d] = links.go(
                block(other, d, piece_cols(h, -d)), near2.at[h, n, :, in_half(-d)], place.ahead(other, d)
            )
    for h, axis, other in ways:
        for n, d in enumerate((1, -1)):
            far[h, d].wait_recv()
            add(block(other, d, piece_cols(h, d)), far2[h, n])
            late[h, d] = links.go(
                block(other, d, piece_cols(h, d)), near2.at[h, n, :, in_half(d)], place.ahead(other, d)
            )
    for h, axis, other in ways:
        for d in (1, -1):
            early[h, d].wait_recv()
            late[h, d].wait_recv()
        total = block(other, 0, half_cols(h))[...] + (near2[h, 0] + near2[h, 1])
        out_ref[:, half_cols(h)] = total.astype(out_ref.dtype)
    run(spread)
    settle(links, place, swap)


def down_projection(hidden, weight, start, collective_id):
    tokens, depth = hidden.shape
    width = weight.shape[1]
    rows = tokens // (2 * RING)
    share_rows, rank = start.shape[0] // RING, start.shape[1]
    copies = 32 + 1 + GATHER_COPIES
    vmem, anywhere = pl.BlockSpec(memory_space=pltpu.VMEM), pl.BlockSpec(memory_space=pl.ANY)
    return pl.pallas_call(
        mlp_kernel,
        out_shape=(jax.ShapeDtypeStruct((rows, width), BF16), spread_shape(share_rows, rank)),
        in_specs=[vmem, anywhere, vmem],
        out_specs=(vmem, anywhere),
        scratch_shapes=[
            pltpu.VMEM((RING, tokens, depth), BF16),
            pltpu.VMEM((depth, width), BF16),
            pltpu.VMEM((RING, RING, 2, rows, width), F32),
            pltpu.VMEM((RING, RING, rows, width), F32),
            pltpu.VMEM((2, 2, RING, rows, width // 4), F32),
            pltpu.VMEM((2, 2, RING, rows, width // 2), F32),
            pltpu.VMEM((2, 2, rows, width // 4), F32),
            pltpu.VMEM((2, 2, rows, width // 2), F32),
            pltpu.VMEM((share_rows + CODE_PAD, rank), jnp.int16),
            pltpu.SemaphoreType.DMA((copies,)),
            pltpu.SemaphoreType.DMA((copies,)),
            pltpu.SemaphoreType.DMA,
            pltpu.SemaphoreType.DMA,
        ],
        compiler_params=pltpu.CompilerParams(collective_id=collective_id, has_side_effects=True),
        name="down_projection",
    )(hidden, weight, start)


def kept_kernel(kept_ref, rows_ref, cols_ref, send, recv, sem):
    place = Place()
    links = Links(send, recv)
    meet(plane_neighbours(place) + y_neighbours(place))
    local = pltpu.make_async_copy(kept_ref, rows_ref.at[by_token(place.z, place.x, place.c)], sem)
    local.start()
    steps = gather_steps(kept_ref, rows_ref, by_token, kept_ref.shape[1], links, place)
    next(steps)
    next(steps)
    local.wait()
    run(steps)
    for made in links.started:
        made.wait_send()
    width = cols_ref.shape[-1]
    start = pl.multiple_of((place.x * 2 + place.c) * width, width)
    source = rows_ref.at[:, :, :, :, pl.ds(start, width)]
    distance = lax.rem(place.t - place.z + RING, RING)
    up, down = place.ahead("t", 1), place.ahead("t", -1)
    to_up = links.copy(source, cols_ref, up)
    to_down = links.copy(source, cols_ref, down)
    low = cols_ref.at[pl.ds(0, RING // 2)]
    high = cols_ref.at[pl.ds(RING // 2, RING // 2)]
    on_up = links.copy(low, low, up)
    on_down = links.copy(high, high, down)

    @pl.when(distance == 0)
    def _():
        to_up.start()
        to_down.start()
        own = pltpu.make_async_copy(source, cols_ref, sem)
        own.start()
        own.wait()
        to_up.wait_send()
        to_down.wait_send()

    @pl.when(distance == 1)
    def _():
        to_up.wait_recv()
        on_up.start()
        on_up.wait_send()

    @pl.when(distance == 3)
    def _():
        to_down.wait_recv()
        on_down.start()
        on_down.wait_send()

    @pl.when(distance == 2)
    def _():
        on_up.wait_recv()
        on_down.wait_recv()


def gather_kept(kept, tile_width, collective_id):
    rows, width = kept.shape
    lead = (RING, RING, 2, rows)
    copies = GATHER_COPIES + 4
    kept_rows, kept_cols = pl.pallas_call(
        kept_kernel,
        out_shape=(
            jax.ShapeDtypeStruct(lead + (width,), kept.dtype),
            jax.ShapeDtypeStruct(lead + (tile_width,), kept.dtype),
        ),
        in_specs=[pl.BlockSpec(memory_space=pltpu.VMEM)],
        out_specs=(pl.BlockSpec(memory_space=pltpu.VMEM), pl.BlockSpec(memory_space=pltpu.VMEM)),
        scratch_shapes=[
            pltpu.SemaphoreType.DMA((copies,)),
            pltpu.SemaphoreType.DMA((copies,)),
            pltpu.SemaphoreType.DMA,
        ],
        compiler_params=pltpu.CompilerParams(collective_id=collective_id, has_side_effects=True),
        name="gather_kept",
    )(kept)
    return kept_rows.reshape(-1, width), kept_cols.reshape(-1, tile_width)


def total_steps(gram_ref, out_ref, scratch, links, place):
    pair, mine, first, second, last, sum_one, sum_two = scratch
    n = gram_ref.shape[0]
    half, width = n // 2, n // 2
    block, piece = half // RING, half // RING // RING
    ways = (("x", "z", pl.ds(0, width)), ("z", "x", pl.ds(width, width)))
    kept_base = pl.multiple_of(place.c * half, half)
    gone_base = pl.multiple_of((1 - place.c) * half, half)
    swapped = links.go(gram_ref.at[pl.ds(gone_base, half)], pair, place.other_core())
    yield
    swapped.wait_recv()
    mine[...] = gram_ref[pl.ds(kept_base, half), :] + pair[...]
    sent = {}
    for p, (axis, other, cols) in enumerate(ways):
        for k in (1, 2, 3):
            start = pl.multiple_of(place.along(axis, k) * block, block)
            sent[p, k] = links.go(
                mine.at[pl.ds(start, block), cols], first.at[p, k - 1], place.ahead(axis, k)
            )
    yield
    for p, (axis, other, cols) in enumerate(ways):
        for k in (1, 2, 3):
            sent[p, k].wait_recv()
        start = pl.multiple_of(getattr(place, axis) * block, block)
        sum_one[p] = (mine[pl.ds(start, block), cols] + first[p, 0]) + (first[p, 1] + first[p, 2])
        for k in (1, 2, 3):
            start = pl.multiple_of(place.along(other, k) * piece, piece)
            sent[p, k] = links.go(
                sum_one.at[p, pl.ds(start, piece)], second.at[p, k - 1], place.ahead(other, k)
            )
    yield
    for p, (axis, other, cols) in enumerate(ways):
        for k in (1, 2, 3):
            sent[p, k].wait_recv()
        start = pl.multiple_of(getattr(place, other) * piece, piece)
        sum_two[p] = (sum_one[p, pl.ds(start, piece), :] + second[p, 0]) + (second[p, 1] + second[p, 2])
        for k in (1, 2, 3):
            sent[p, k] = links.go(sum_two.at[p], last.at[p, place.t], place.ahead("t", k))
        last[p, pl.ds(place.t, 1)] = sum_two[p][None]
    yield
    for p, (axis, other, cols) in enumerate(ways):
        for k in (1, 2, 3):
            sent[p, k].wait_recv()
        base = kept_base + getattr(place, axis) * block
        start = pl.multiple_of(base + getattr(place, other) * piece, piece)
        final = out_ref.at[pl.ds(start, piece), cols]
        final[...] = (last[p, 0] + last[p, 1]) + (last[p, 2] + last[p, 3])
        for k in (1, 2, 3):
            sent[p, k] = links.go(final, final, place.ahead(other, k))
    yield
    for p, (axis, other, cols) in enumerate(ways):
        for k in (1, 2, 3):
            sent[p, k].wait_recv()
        start = pl.multiple_of(kept_base + getattr(place, axis) * block, block)
        whole = out_ref.at[pl.ds(start, block), cols]
        for k in (1, 2, 3):
            sent[p, k] = links.go(whole, whole, place.ahead(axis, k))
    yield
    for p in range(2):
        for k in (1, 2, 3):
            sent[p, k].wait_recv()
    side = out_ref.at[pl.ds(kept_base, half)]
    across = links.go(side, side, place.other_core())
    yield
    across.wait_recv()


TOTAL_COPIES = 32


def total_scratch(n):
    block, piece = n // 2 // RING, n // 2 // RING // RING
    return [
        pltpu.VMEM((n // 2, n), F32),
        pltpu.VMEM((n // 2, n), F32),
        pltpu.VMEM((2, 3, block, n // 2), F32),
        pltpu.VMEM((2, 3, piece, n // 2), F32),
        pltpu.VMEM((2, RING, piece, n // 2), F32),
        pltpu.VMEM((2, block, n // 2), F32),
        pltpu.VMEM((2, piece, n // 2), F32),
    ]


def everyone(place):
    return [place.other_core()] + [
        place.ahead(axis, k) for axis in ("x", "z", "t") for k in (1, 2, 3)
    ]


def gram_of(rows):
    return lax.dot_general(
        rows, rows, (((0,), (0,)), ((), ())), precision=HIGH, preferred_element_type=F32
    )


def first_image_kernel(part_ref, out_ref, total_ref, share, gram, codes, *refs):
    relay, build, arrive = refs[:3]
    scratch = refs[3:10]
    send, recv, sem = refs[10:]
    place = Place()
    links = Links(send, recv)
    meet(everyone(place), place)
    reduce_y(part_ref, share, relay, build, arrive, links, place)
    known = encode(share[...], codes)
    swap = swap_start(codes, out_ref, links, place, sem)
    gram[...] = gram_of(known)
    total = total_steps(gram, total_ref, scratch, links, place)
    next(total)
    swap_end(swap, place)
    spread = spread_steps(codes, out_ref, links, place)
    next(spread)
    next(total)
    next(spread)
    next(total)
    next(spread)
    next(total)
    next(total)
    next(spread)
    next(total)
    next(spread)
    run(total)
    run(spread)
    settle(links, place, swap)


def first_image(part, collective_id):
    rows, width = part.shape[0] // RING, part.shape[1]
    copies = REDUCE_COPIES + 1 + GATHER_COPIES + TOTAL_COPIES
    vmem = pl.BlockSpec(memory_space=pltpu.VMEM)
    return pl.pallas_call(
        first_image_kernel,
        out_shape=(spread_shape(rows, width), jax.ShapeDtypeStruct((width, width), F32)),
        in_specs=[vmem],
        out_specs=(pl.BlockSpec(memory_space=pl.ANY), vmem),
        scratch_shapes=[
            pltpu.VMEM((rows, width), F32),
            pltpu.VMEM((width, width), F32),
            pltpu.VMEM((rows + CODE_PAD, width), jnp.int16),
        ]
        + reduce_scratch(rows, width)
        + total_scratch(width)
        + [
            pltpu.SemaphoreType.DMA((copies,)),
            pltpu.SemaphoreType.DMA((copies,)),
            pltpu.SemaphoreType.DMA,
        ],
        compiler_params=pltpu.CompilerParams(collective_id=collective_id, has_side_effects=True),
        name="first_image",
    )(part)


def second_image_kernel(part_ref, inverse_ref, rows_ref, total_ref, share, gram, *refs):
    relay, build, arrive = refs[:3]
    scratch = refs[3:10]
    send, recv = refs[10:]
    place = Place()
    links = Links(send, recv)
    meet(everyone(place))
    reduce_y(part_ref, share, relay, build, arrive, links, place)
    image = times_transpose(share[...], inverse_ref[...])
    rows_ref[pl.ds(place.t, 1)] = image[None]
    gram[...] = gram_of(image)
    total = total_steps(gram, total_ref, scratch, links, place)
    next(total)
    next(total)
    own = rows_ref.at[place.t]
    around = [links.go(own, own, place.ahead("t", d)) for d in (1, -1)]
    next(total)
    next(total)
    next(total)
    half = image.shape[0] // 2
    onward = []
    for d, made in zip((1, -1), around):
        made.wait_recv()
        held = rows_ref.at[place.along("t", -d), pl.ds(0 if d > 0 else half, half)]
        onward.append(links.go(held, held, place.ahead("t", d)))
    run(total)
    for made in onward:
        made.wait_recv()
    settle(links, place)


def second_image(part, inverse, collective_id):
    rows, width = part.shape[0] // RING, part.shape[1]
    copies = REDUCE_COPIES + TOTAL_COPIES + 4
    vmem = pl.BlockSpec(memory_space=pltpu.VMEM)
    out, total = pl.pallas_call(
        second_image_kernel,
        out_shape=(
            jax.ShapeDtypeStruct((RING, rows, width), F32),
            jax.ShapeDtypeStruct((width, width), F32),
        ),
        in_specs=[vmem, vmem],
        out_specs=(vmem, vmem),
        scratch_shapes=[pltpu.VMEM((rows, width), F32), pltpu.VMEM((width, width), F32)]
        + reduce_scratch(rows, width)
        + total_scratch(width)
        + [pltpu.SemaphoreType.DMA((copies,)), pltpu.SemaphoreType.DMA((copies,))],
        compiler_params=pltpu.CompilerParams(collective_id=collective_id, has_side_effects=True),
        name="second_image",
    )(part, inverse)
    return out.reshape(-1, width), total


def body(hidden, down_weight, covariance, keep_index, start_basis):
    fsdp_count = lax.axis_size("fsdp")
    total_tokens = TOK_DEV * fsdp_count
    block_width = covariance.shape[1]
    f = lax.axis_index("fsdp")
    root = math.sqrt(D)

    mlp_out, start_codes = down_projection(hidden, down_weight, start_basis, 0)
    listed = keep_index[0]
    positions = jnp.arange(mlp_out.shape[0], dtype=jnp.int32)
    chosen = (listed[:, None] == positions[None, :]).astype(BF16)
    kept = jnp.dot(chosen, mlp_out, preferred_element_type=F32).astype(BF16)
    kept_pair = gather_kept(kept, block_width, 2)
    new_covariance, part_one = image_part(covariance, start_codes, kept_pair, 1.0 / total_tokens)
    codes_one, total_one = first_image(part_one, 1)
    inverse_one = inverse_factor(total_one)
    every = codes_one.reshape(fsdp_count, -1, codes_one.shape[-1])
    own_rows = decode(lax.dynamic_index_in_dim(every, f, 0, keepdims=False))
    first_basis = times_transpose(own_rows, inverse_one, root)
    whole_two, total_two = second_image(image_part(new_covariance, codes_one), inverse_one, 3)
    final_basis = times_transpose(whole_two, inverse_factor(total_two), root)
    return (mlp_out, new_covariance, first_basis, final_basis)


def solution(mesh):
    placed = (
        P("tensor", "fsdp"),
        P("fsdp", "tensor"),
        P("tensor", "fsdp"),
        P("fsdp", None),
        P("fsdp", None),
    )
    return jax.shard_map(
        body,
        mesh=mesh,
        in_specs=placed,
        out_specs=(
            P("fsdp", "tensor"),
            P("tensor", "fsdp"),
            P(("tensor", "fsdp"), None),
            P("fsdp", None),
        ),
        check_vma=False,
    )
```

```python
import functools
import math

import jax
import jax.numpy as jnp
from jax import lax
from jax.experimental import pallas as pl
from jax.experimental.pallas import tpu as pltpu
from jax.sharding import PartitionSpec as P

D = 16384
TOK_DEV = 16
F32 = jnp.float32
BF16 = jnp.bfloat16
HIGH = lax.Precision.HIGH


def inverse_factor_kernel(scale, gram_ref, *refs):
    rows_ref, out_ref = refs[0], refs[-4]
    scaled, work, state = refs[-3:]
    n = gram_ref.shape[0]
    rows = lax.broadcasted_iota(jnp.int32, (n, n), 0)
    cols = lax.broadcasted_iota(jnp.int32, (n, n), 1)
    gram = gram_ref[...]
    diagonal = jnp.where(rows == cols, gram, 0.0)
    col_scale = lax.rsqrt(jnp.sum(diagonal, axis=1, keepdims=True))
    row_scale = lax.rsqrt(jnp.sum(diagonal, axis=0, keepdims=True))
    scaled[...] = gram * col_scale * row_scale

    def half_lower(residual):
        return jnp.where(rows > cols, residual, jnp.where(rows == cols, 0.5 * residual, 0.0))

    def residual_of(x, precision):
        left = jnp.dot(x, scaled[...], precision=precision, preferred_element_type=F32)
        full = lax.dot_general(
            left, x, (((1,), (1,)), ((), ())), precision=precision, preferred_element_type=F32
        )
        return full - jnp.where(rows == cols, 1.0, 0.0)

    eye = jnp.where(rows == cols, 1.0, 0.0)
    work[...] = eye - half_lower(scaled[...] - eye)

    @pl.loop(0, 2)
    def _(step):
        x = work[...]
        residual = residual_of(x, None)
        work[...] = x - jnp.dot(half_lower(residual), x, preferred_element_type=F32)

    state[0] = 1.0

    def unfinished(step):
        error = state[0]
        return jnp.logical_and(step < 12, jnp.logical_not(error < 1e-3))

    def refine(step):
        x = work[...]
        residual = residual_of(x, HIGH)
        work[...] = x - jnp.dot(half_lower(residual), x, preferred_element_type=F32)
        state[0] = jnp.sum(residual * residual)
        return step + 1

    lax.while_loop(unfinished, refine, 0)

    @pl.when(jnp.logical_not(state[0] < 1e-3))
    def _():
        work[...] = eye

        @pl.loop(0, n)
        def _(j):
            here = cols[0:1] == j
            pivot_row = scaled[pl.ds(j, 1), :]
            pivot = lax.rsqrt(jnp.sum(jnp.where(here, pivot_row, 0.0), axis=1, keepdims=True))
            left = jnp.sum(jnp.where(cols == j, scaled[...], 0.0), axis=1, keepdims=True) * pivot
            left = jnp.where(rows[:, 0:1] > j, left, 0.0)
            own = work[pl.ds(j, 1), :] * pivot
            scaled[...] = scaled[...] - left * (pivot_row * pivot)
            work[...] = work[...] - left * own
            work[pl.ds(j, 1), :] = own

    inverse = work[...] * row_scale
    if scale is None:
        out_ref[...] = inverse
    else:
        out_ref[...] = times_transpose(rows_ref[...], inverse, scale)


def inverse_factor(gram, rows=None, scale=None):
    n = gram.shape[0]
    operands = (gram,) if rows is None else (gram, rows)
    return pl.pallas_call(
        functools.partial(inverse_factor_kernel, scale),
        out_shape=jax.ShapeDtypeStruct(operands[-1].shape, F32),
        in_specs=[pl.BlockSpec(memory_space=pltpu.VMEM)] * len(operands),
        out_specs=pl.BlockSpec(memory_space=pltpu.VMEM),
        scratch_shapes=[pltpu.VMEM((n, n), F32), pltpu.VMEM((n, n), F32), pltpu.SMEM((1,), F32)],
        cost_estimate=pl.CostEstimate(flops=8_000_000_000, bytes_accessed=2 << 20, transcendentals=0),
        name="inverse_factor",
    )(*operands)


def times_transpose(rows, factor, scale=1.0):
    out = lax.dot_general(
        rows, factor, (((1,), (1,)), ((), ())), precision=HIGH, preferred_element_type=F32
    )
    return out * scale if scale != 1.0 else out


MESH = pl.DeviceIdType.MESH
RING = 4


class Place:
    def __init__(self):
        f = lax.axis_index("fsdp")
        self.t = lax.axis_index("tensor")
        self.c = lax.rem(f, 2)
        self.x = lax.rem(lax.div(f, 2), RING)
        self.z = lax.div(f, 2 * RING)

    def along(self, axis, step):
        return lax.rem(getattr(self, axis) + (step + RING), RING)

    def device(self, **moved):
        at = {name: moved.get(name, getattr(self, name)) for name in ("z", "x", "c", "t")}
        return {"fsdp": (at["z"] * RING + at["x"]) * 2 + at["c"], "tensor": at["t"]}

    def ahead(self, axis, step):
        return self.device(**{axis: self.along(axis, step)})

    def other_core(self):
        return self.device(c=1 - self.c)


def meet(devices, place=None):
    barrier = pltpu.get_barrier_semaphore()
    for device in devices:
        pl.semaphore_signal(barrier, inc=1, device_id=device, device_id_type=MESH)
    count = len(devices)
    if place is not None:

        @pl.when(place.t != place.z)
        def _():
            pl.semaphore_signal(
                barrier, inc=1, device_id=place.device(z=place.t, t=place.z), device_id_type=MESH
            )

        count = count + jnp.where(place.t != place.z, 1, 0)
    pl.semaphore_wait(barrier, count)


class Links:
    def __init__(self, send, recv):
        self.send, self.recv, self.started = send, recv, []

    def copy(self, src, dst, device):
        i = len(self.started)
        made = pltpu.make_async_remote_copy(
            src_ref=src,
            dst_ref=dst,
            send_sem=self.send.at[i],
            recv_sem=self.recv.at[i],
            device_id=device,
            device_id_type=MESH,
        )
        self.started.append(made)
        return made

    def go(self, src, dst, device):
        made = self.copy(src, dst, device)
        made.start()
        return made


def gather_steps(own, out, slot, width, links, place):
    half, piece = width // 2, width // 4
    ways = ((0, "x", "z"), (1, "z", "x"))

    def at(z, x, cols):
        return out.at[slot(z, x, place.c) + (slice(None), cols)]

    def spot(axis, step, cols):
        z = place.along("z", step) if axis == "z" else place.z
        x = place.along("x", step) if axis == "x" else place.x
        return at(z, x, cols)

    def line(axis, other, step, cols):
        if axis == "x":
            return at(place.along(other, step), slice(None), cols)
        return at(slice(None), place.along(other, step), cols)

    def half_cols(h):
        return pl.ds(h * half, half)

    def piece_cols(h, d):
        return pl.ds(h * half + (0 if d > 0 else piece), piece)

    made, rest = {}, []
    for h, axis, _ in ways:
        for d in (1, -1):
            cols = half_cols(h)
            made[h, d] = links.go(own.at[:, cols], spot(axis, 0, cols), place.ahead(axis, d))
    yield
    onward = {}
    for h, axis, _ in ways:
        for d in (1, -1):
            made[h, d].wait_recv()
            chunk = spot(axis, -d, piece_cols(h, d))
            onward[h, d] = links.go(chunk, chunk, place.ahead(axis, d))
    yield
    for h, axis, other in ways:
        for d in (1, -1):
            onward[h, d].wait_recv()
        whole = line(axis, other, 0, half_cols(h))
        for d in (1, -1):
            made[h, d] = links.go(whole, whole, place.ahead(other, d))
        rest.append(links.go(whole, whole, place.other_core()))
    yield
    for h, axis, other in ways:
        for d in (1, -1):
            made[h, d].wait_recv()
            part = line(axis, other, -d, piece_cols(h, d))
            onward[h, d] = links.go(part, part, place.ahead(other, d))
            whole = line(axis, other, -d, half_cols(h))
            rest.append(links.go(whole, whole, place.other_core()))
    yield
    for h, axis, other in ways:
        for d in (1, -1):
            onward[h, d].wait_recv()
            part = line(axis, other, -2 * d, piece_cols(h, d))
            rest.append(links.go(part, part, place.other_core()))
    yield
    for made_last in rest:
        made_last.wait_recv()


def run(steps):
    for _ in steps:
        pass


GATHER_COPIES = 26


def plane_neighbours(place):
    return [place.ahead(axis, d) for axis in ("x", "z") for d in (1, -1)] + [place.other_core()]


def by_column(z, x, c):
    return (x, c, z)


def by_token(z, x, c):
    return (z, x, c)


def swap_start(share, out, links, place, sem):
    sent = links.copy(
        share, out.at[by_column(place.t, place.x, place.c)], place.device(z=place.t, t=place.z)
    )
    kept = pltpu.make_async_copy(share, out.at[by_column(place.z, place.x, place.c)], sem)

    @pl.when(place.t != place.z)
    def _():
        sent.start()

    @pl.when(place.t == place.z)
    def _():
        kept.start()

    return sent, kept


def swap_end(swap, place):
    sent, kept = swap

    @pl.when(place.t != place.z)
    def _():
        sent.wait_recv()

    @pl.when(place.t == place.z)
    def _():
        kept.wait()


def settle(links, place, swap=None):
    for made in links.started:
        if swap is not None and made is swap[0]:

            @pl.when(place.t != place.z)
            def _():
                made.wait_send()
        else:
            made.wait_send()


CODE_PAD = 16


def encode(share, codes):
    rows = share.shape[0]
    largest = jnp.maximum(jnp.max(jnp.abs(share), axis=0, keepdims=True), 1e-30)
    exponent = jnp.ceil(jnp.log2(largest) - 14.99)
    scaled = jnp.clip(jnp.round(share * jnp.exp2(-exponent)), -32767.0, 32767.0)
    codes[pl.ds(0, rows), :] = scaled.astype(jnp.int32).astype(jnp.int16)
    marks = jnp.broadcast_to(exponent.astype(jnp.int32), (CODE_PAD, share.shape[1]))
    codes[pl.ds(rows, CODE_PAD), :] = marks.astype(jnp.int16)
    return scaled * jnp.exp2(exponent)


def decode(codes):
    wide = codes.astype(jnp.int32).astype(F32)
    rows = codes.shape[0] - CODE_PAD
    return wide[:rows] * jnp.exp2(wide[rows : rows + 1])


def spread_shape(rows, width):
    return jax.ShapeDtypeStruct((RING, 2, RING, rows + CODE_PAD, width), jnp.int16)


def spread_steps(codes, out_ref, links, place):
    own = out_ref.at[by_column(place.z, place.x, place.c)]
    return gather_steps(own, out_ref, by_column, codes.shape[1], links, place)


HALVES = 2


def reduce_steps(part_ref, share_ref, scratch, h, links, place):
    relay, build, arrive = scratch
    rows, width = share_ref.shape[0], share_ref.shape[1] // HALVES
    half = width // 2
    low, high = pl.ds(0, half), pl.ds(half, half)

    def quarter(step, offset, size):
        start = pl.multiple_of(place.along("t", step) * rows, rows)
        return part_ref.at[pl.ds(start, rows), pl.ds(h * width + offset, size)]

    up, down = place.ahead("t", 1), place.ahead("t", -1)
    far_up = links.go(quarter(2, 0, half), relay.at[h, 0], up)
    far_down = links.go(quarter(2, half, half), relay.at[h, 1], down)
    near_up = links.go(quarter(1, half, half), arrive.at[h, 0, :, high], up)
    near_down = links.go(quarter(-1, 0, half), arrive.at[h, 1, :, low], down)
    yield
    far_up.wait_recv()
    build[h, 0] = quarter(1, 0, half)[...] + relay[h, 0]
    sum_up = links.go(build.at[h, 0], arrive.at[h, 0, :, low], up)
    far_down.wait_recv()
    build[h, 1] = quarter(-1, half, half)[...] + relay[h, 1]
    sum_down = links.go(build.at[h, 1], arrive.at[h, 1, :, high], down)
    yield
    for made in (near_up, near_down, sum_up, sum_down):
        made.wait_recv()
    share_ref[:, pl.ds(h * width, width)] = quarter(0, 0, width)[...] + (arrive[h, 0] + arrive[h, 1])


REDUCE_COPIES = 6 * HALVES


def reduce_scratch(rows, width):
    return [
        pltpu.VMEM((HALVES, 2, rows, width // HALVES // 2), F32),
        pltpu.VMEM((HALVES, 2, rows, width // HALVES // 2), F32),
        pltpu.VMEM((HALVES, 2, rows, width // HALVES), F32),
    ]


def y_neighbours(place):
    return [place.ahead("t", 1), place.ahead("t", -1)]


def image_block(tile, codes):
    rows = jnp.concatenate(
        [decode(codes[i, j]) for i in range(codes.shape[0]) for j in range(codes.shape[1])], axis=0
    )
    return lax.dot_general(
        tile, rows, (((0,), (0,)), ((), ())), precision=HIGH, preferred_element_type=F32
    )


def update_kernel(scale, tile_ref, codes_ref, kept_rows_ref, kept_cols_ref, new_ref, out_ref):
    update = lax.dot_general(
        kept_rows_ref[...], kept_cols_ref[...], (((0,), (0,)), ((), ())), preferred_element_type=F32
    )
    tile = tile_ref[...] + update * scale
    new_ref[...] = tile
    part = image_block(tile, codes_ref[0])

    @pl.when(pl.program_id(0) == 0)
    def _():
        out_ref[...] = part

    @pl.when(pl.program_id(0) > 0)
    def _():
        out_ref[...] += part


def update_and_image(tile, codes, kept_rows, kept_cols, scale):
    width, rank = tile.shape[1], codes.shape[4]
    tokens = kept_rows.shape[0]
    height = tile.shape[0] // RING
    tile_spec = pl.BlockSpec((height, width), lambda i: (i, 0))
    return pl.pallas_call(
        functools.partial(update_kernel, scale),
        grid=(RING,),
        out_shape=(
            jax.ShapeDtypeStruct(tile.shape, F32),
            jax.ShapeDtypeStruct((width, rank), F32),
        ),
        in_specs=[
            tile_spec,
            pl.BlockSpec((1,) + codes.shape[1:], lambda i: (i, 0, 0, 0, 0)),
            pl.BlockSpec((tokens, height), lambda i: (0, i)),
            pl.BlockSpec(kept_cols.shape, lambda i: (0, 0)),
        ],
        out_specs=(tile_spec, pl.BlockSpec((width, rank), lambda i: (0, 0))),
        name="update_image",
    )(tile, codes, kept_rows, kept_cols)


def columns_along_y(rows_ref, cols_ref, links, place, sem):
    width = cols_ref.shape[-1]
    start = pl.multiple_of((place.x * 2 + place.c) * width, width)
    source = rows_ref.at[:, :, :, :, pl.ds(start, width)]
    distance = lax.rem(place.t - place.z + RING, RING)
    up, down = place.ahead("t", 1), place.ahead("t", -1)
    to_up = links.copy(source, cols_ref, up)
    to_down = links.copy(source, cols_ref, down)
    low = cols_ref.at[pl.ds(0, RING // 2)]
    high = cols_ref.at[pl.ds(RING // 2, RING // 2)]
    on_up = links.copy(low, low, up)
    on_down = links.copy(high, high, down)

    @pl.when(distance == 0)
    def _():
        to_up.start()
        to_down.start()
        own = pltpu.make_async_copy(source, cols_ref, sem)
        own.start()
        own.wait()
        to_up.wait_send()
        to_down.wait_send()

    @pl.when(distance == 1)
    def _():
        to_up.wait_recv()
        on_up.start()
        on_up.wait_send()

    @pl.when(distance == 3)
    def _():
        to_down.wait_recv()
        on_down.start()
        on_down.wait_send()

    @pl.when(distance == 2)
    def _():
        on_up.wait_recv()
        on_down.wait_recv()


def mlp_kernel(
    hidden_ref,
    weight_ref,
    start_ref,
    keep_ref,
    out_ref,
    spread_ref,
    rows_ref,
    cols_ref,
    hid,
    weight,
    part,
    pair,
    far1,
    near1,
    far2,
    near2,
    codes,
    send,
    recv,
    sem,
    swap_sem,
    cols_sem,
):
    place = Place()
    links = Links(send, recv)
    load = pltpu.make_async_copy(weight_ref, weight, sem)
    load.start()
    meet(plane_neighbours(place) + y_neighbours(place), place)
    tokens = hidden_ref.shape[0]
    width = weight.shape[1]
    half, piece, tile = width // 2, width // 4, 512
    up, down = place.ahead("t", 1), place.ahead("t", -1)
    c = place.c
    to_up = links.go(hidden_ref, hid.at[place.t], up)
    to_down = links.go(hidden_ref, hid.at[place.t], down)
    share_rows = codes.shape[0] - CODE_PAD
    share_start = pl.multiple_of(place.t * share_rows, share_rows)
    encode(start_ref[pl.ds(share_start, share_rows), :], codes)
    swap = swap_start(codes, spread_ref, links, place, swap_sem)
    load.wait()

    def product(group, rows):
        @pl.loop(0, width // tile)
        def _(j):
            cols = pl.ds(pl.multiple_of(j * tile, tile), tile)
            block = jnp.dot(rows[...], weight[:, cols], preferred_element_type=F32)
            part[group, :, :, :, cols] = block.reshape(RING, 2, tokens // (2 * RING), tile)

        return links.go(part.at[group, :, 1 - c], pair.at[group], place.other_core())

    pairs = [product(place.t, hidden_ref)]
    below, above, across = place.along("t", -1), place.along("t", 1), place.along("t", 2)
    to_up.wait_recv()
    first = hid.at[below, pl.ds(0, tokens // 2)]
    on_up = links.go(first, first, up)
    to_down.wait_recv()
    second = hid.at[above, pl.ds(tokens // 2, tokens // 2)]
    on_down = links.go(second, second, down)
    pairs.append(product(below, hid.at[below]))
    swap_end(swap, place)
    spread = spread_steps(codes, spread_ref, links, place)
    next(spread)
    pairs.append(product(above, hid.at[above]))
    on_up.wait_recv()
    on_down.wait_recv()
    pairs.append(product(across, hid.at[across]))
    next(spread)
    for group, made in zip((place.t, below, above, across), pairs):
        made.wait_recv()

        @pl.loop(0, RING)
        def _(i):
            part[group, i, c] = part[group, i, c] + pair[group, i]

    ways = ((0, "z", "x"), (1, "x", "z"))

    def half_cols(h):
        return pl.ds(h * half, half)

    def piece_cols(h, d):
        return pl.ds(h * half + (0 if d > 0 else piece), piece)

    def in_half(d):
        return pl.ds(0 if d > 0 else piece, piece)

    def line(axis, step, cols, i=slice(None)):
        if axis == "z":
            return part.at[place.along("z", step), i, c, :, cols]
        return part.at[i, place.along("x", step), c, :, cols]

    def block(other, step, cols):
        if other == "z":
            return part.at[place.along("z", step), place.x, c, :, cols]
        return part.at[place.z, place.along("x", step), c, :, cols]

    def add(into, value):
        into[...] = into[...] + value

    far, early, late = {}, {}, {}
    for h, axis, _ in ways:
        for n, d in enumerate((1, -1)):
            far[h, d] = links.go(line(axis, 2, piece_cols(h, d)), far1.at[h, n], place.ahead(axis, d))
    for h, axis, _ in ways:
        for n, d in enumerate((1, -1)):
            early[h, d] = links.go(
                line(axis, d, piece_cols(h, -d)), near1.at[h, n, :, :, in_half(-d)], place.ahead(axis, d)
            )
    next(spread)
    for h, axis, _ in ways:
        for n, d in enumerate((1, -1)):
            far[h, d].wait_recv()

            @pl.loop(0, RING)
            def _(i):
                add(line(axis, d, piece_cols(h, d), i), far1[h, n, i])

            late[h, d] = links.go(
                line(axis, d, piece_cols(h, d)), near1.at[h, n, :, :, in_half(d)], place.ahead(axis, d)
            )
    next(spread)
    for h, axis, other in ways:
        for d in (1, -1):
            early[h, d].wait_recv()
            late[h, d].wait_recv()

        @pl.loop(0, RING)
        def _(i):
            add(line(axis, 0, half_cols(h), i), near1[h, 0, i] + near1[h, 1, i])

        for n, d in enumerate((1, -1)):
            far[h, d] = links.go(block(other, 2, piece_cols(h, d)), far2.at[h, n], place.ahead(other, d))
        for n, d in enumerate((1, -1)):
            early[h, d] = links.go(
                block(other, d, piece_cols(h, -d)), near2.at[h, n, :, in_half(-d)], place.ahead(other, d)
            )
    for h, axis, other in ways:
        for n, d in enumerate((1, -1)):
            far[h, d].wait_recv()
            add(block(other, d, piece_cols(h, d)), far2[h, n])
            late[h, d] = links.go(
                block(other, d, piece_cols(h, d)), near2.at[h, n, :, in_half(d)], place.ahead(other, d)
            )
    next(spread)
    for h, axis, other in ways:
        for d in (1, -1):
            early[h, d].wait_recv()
            late[h, d].wait_recv()
        total = block(other, 0, half_cols(h))[...] + (near2[h, 0] + near2[h, 1])
        out_ref[:, half_cols(h)] = total.astype(out_ref.dtype)
    places = lax.broadcasted_iota(jnp.int32, (out_ref.shape[0], keep_ref.shape[1]), 0)
    chosen = jnp.where(places == keep_ref[...], 1.0, 0.0).astype(BF16)
    kept = lax.dot_general(
        chosen, out_ref[...], (((0,), (0,)), ((), ())), preferred_element_type=F32
    )
    rows_ref[place.z, place.x, place.c] = kept.astype(BF16)
    own = rows_ref.at[by_token(place.z, place.x, place.c)]
    run(gather_steps(own, rows_ref, by_token, width, links, place))
    run(spread)
    settle(links, place, swap)
    columns_along_y(rows_ref, cols_ref, links, place, cols_sem)


def down_projection(hidden, weight, start, keep_index, tile_width, collective_id):
    tokens, depth = hidden.shape
    width = weight.shape[1]
    rows = tokens // (2 * RING)
    share_rows, rank = start.shape[0] // RING, start.shape[1]
    copies = 32 + 1 + 2 * GATHER_COPIES + 4
    lead = (RING, RING, 2, keep_index.shape[1])
    vmem, anywhere = pl.BlockSpec(memory_space=pltpu.VMEM), pl.BlockSpec(memory_space=pl.ANY)
    return pl.pallas_call(
        mlp_kernel,
        out_shape=(
            jax.ShapeDtypeStruct((rows, width), BF16),
            spread_shape(share_rows, rank),
            jax.ShapeDtypeStruct(lead + (width,), BF16),
            jax.ShapeDtypeStruct(lead + (tile_width,), BF16),
        ),
        in_specs=[vmem, anywhere, vmem, vmem],
        out_specs=(vmem, anywhere, vmem, vmem),
        scratch_shapes=[
            pltpu.VMEM((RING, tokens, depth), BF16),
            pltpu.VMEM((depth, width), BF16),
            pltpu.VMEM((RING, RING, 2, rows, width), F32),
            pltpu.VMEM((RING, RING, rows, width), F32),
            pltpu.VMEM((2, 2, RING, rows, width // 4), F32),
            pltpu.VMEM((2, 2, RING, rows, width // 2), F32),
            pltpu.VMEM((2, 2, rows, width // 4), F32),
            pltpu.VMEM((2, 2, rows, width // 2), F32),
            pltpu.VMEM((share_rows + CODE_PAD, rank), jnp.int16),
            pltpu.SemaphoreType.DMA((copies,)),
            pltpu.SemaphoreType.DMA((copies,)),
            pltpu.SemaphoreType.DMA,
            pltpu.SemaphoreType.DMA,
            pltpu.SemaphoreType.DMA,
        ],
        compiler_params=pltpu.CompilerParams(collective_id=collective_id, has_side_effects=True),
        name="down_projection",
    )(hidden, weight, start, keep_index)


def total_steps(gram_ref, out_ref, scratch, links, place):
    pair, mine, first, second, last, sum_one, sum_two = scratch
    n = gram_ref.shape[0]
    half, width = n // 2, n // 2
    block, piece = half // RING, half // RING // RING
    ways = (("x", "z", pl.ds(0, width)), ("z", "x", pl.ds(width, width)))
    kept_base = pl.multiple_of(place.c * half, half)
    gone_base = pl.multiple_of((1 - place.c) * half, half)
    swapped = links.go(gram_ref.at[pl.ds(gone_base, half)], pair, place.other_core())
    yield
    swapped.wait_recv()
    mine[...] = gram_ref[pl.ds(kept_base, half), :] + pair[...]
    sent = {}
    for p, (axis, other, cols) in enumerate(ways):
        for k in (1, 2, 3):
            start = pl.multiple_of(place.along(axis, k) * block, block)
            sent[p, k] = links.go(
                mine.at[pl.ds(start, block), cols], first.at[p, k - 1], place.ahead(axis, k)
            )
    yield
    for p, (axis, other, cols) in enumerate(ways):
        for k in (1, 2, 3):
            sent[p, k].wait_recv()
        start = pl.multiple_of(getattr(place, axis) * block, block)
        sum_one[p] = (mine[pl.ds(start, block), cols] + first[p, 0]) + (first[p, 1] + first[p, 2])
        for k in (1, 2, 3):
            start = pl.multiple_of(place.along(other, k) * piece, piece)
            sent[p, k] = links.go(
                sum_one.at[p, pl.ds(start, piece)], second.at[p, k - 1], place.ahead(other, k)
            )
    yield
    for p, (axis, other, cols) in enumerate(ways):
        for k in (1, 2, 3):
            sent[p, k].wait_recv()
        start = pl.multiple_of(getattr(place, other) * piece, piece)
        sum_two[p] = (sum_one[p, pl.ds(start, piece), :] + second[p, 0]) + (second[p, 1] + second[p, 2])
        for k in (1, 2, 3):
            sent[p, k] = links.go(sum_two.at[p], last.at[p, place.t], place.ahead("t", k))
        last[p, pl.ds(place.t, 1)] = sum_two[p][None]
    yield
    for p, (axis, other, cols) in enumerate(ways):
        for k in (1, 2, 3):
            sent[p, k].wait_recv()
        base = kept_base + getattr(place, axis) * block
        start = pl.multiple_of(base + getattr(place, other) * piece, piece)
        final = out_ref.at[pl.ds(start, piece), cols]
        final[...] = (last[p, 0] + last[p, 1]) + (last[p, 2] + last[p, 3])
        for k in (1, 2, 3):
            sent[p, k] = links.go(final, final, place.ahead(other, k))
    yield
    for p, (axis, other, cols) in enumerate(ways):
        for k in (1, 2, 3):
            sent[p, k].wait_recv()
        start = pl.multiple_of(kept_base + getattr(place, axis) * block, block)
        whole = out_ref.at[pl.ds(start, block), cols]
        for k in (1, 2, 3):
            sent[p, k] = links.go(whole, whole, place.ahead(axis, k))
    yield
    for p in range(2):
        for k in (1, 2, 3):
            sent[p, k].wait_recv()
    side = out_ref.at[pl.ds(kept_base, half)]
    across = links.go(side, side, place.other_core())
    yield
    across.wait_recv()


TOTAL_COPIES = 32


def total_scratch(n):
    block, piece = n // 2 // RING, n // 2 // RING // RING
    return [
        pltpu.VMEM((n // 2, n), F32),
        pltpu.VMEM((n // 2, n), F32),
        pltpu.VMEM((2, 3, block, n // 2), F32),
        pltpu.VMEM((2, 3, piece, n // 2), F32),
        pltpu.VMEM((2, RING, piece, n // 2), F32),
        pltpu.VMEM((2, block, n // 2), F32),
        pltpu.VMEM((2, piece, n // 2), F32),
    ]


def everyone(place):
    return [place.other_core()] + [
        place.ahead(axis, k) for axis in ("x", "z", "t") for k in (1, 2, 3)
    ]


def gram_of(rows):
    return lax.dot_general(
        rows, rows, (((0,), (0,)), ((), ())), precision=HIGH, preferred_element_type=F32
    )


def images_kernel(part_ref, tile_ref, own_ref, share_ref, total_ref, first, gram, codes, every, tile, part, *refs):
    reduce_one, reduce_two, scratch = refs[:3], refs[3:6], refs[6:13]
    send, recv, swap_sem, tile_sem = refs[13:]
    place = Place()
    links = Links(send, recv)
    load = pltpu.make_async_copy(tile_ref, tile, tile_sem)
    load.start()
    meet(everyone(place), place)
    halves = [reduce_steps(part_ref, first, reduce_one, h, links, place) for h in range(HALVES)]
    for _ in range(2):
        for half in halves:
            next(half)
    for half in halves:
        run(half)
    known = encode(first[...], codes)
    swap = swap_start(codes, every, links, place, swap_sem)
    gram[...] = gram_of(known)
    total = total_steps(gram, total_ref, scratch, links, place)
    next(total)
    swap_end(swap, place)
    spread = spread_steps(codes, every, links, place)
    next(spread)
    next(total)
    next(spread)
    next(spread)
    next(total)
    next(total)
    next(total)
    next(spread)
    next(total)
    next(spread)
    load.wait()
    run(spread)
    index = (place.z * RING + place.x) * 2 + place.c
    own_ref[...] = every[lax.div(index, 2 * RING), lax.rem(lax.div(index, RING), 2), lax.rem(index, RING)]
    height = tile.shape[0] // RING
    width = part.shape[1] // HALVES

    def product(h):
        cols = pl.ds(h * width, width)
        part[:, cols] = jnp.zeros((part.shape[0], width), F32)

        @pl.loop(0, RING)
        def _(i):
            rows = tile[pl.ds(pl.multiple_of(i * height, height), height), :]
            part[:, cols] = part[:, cols] + image_block(rows, every[i, :, :, :, cols])

    halves = [reduce_steps(part, share_ref, reduce_two, h, links, place) for h in range(HALVES)]
    product(0)
    next(halves[0])
    next(total)
    product(1)
    next(halves[1])
    next(halves[0])
    run(total)
    next(halves[1])
    for half in halves:
        run(half)
    settle(links, place, swap)


def images(part, tile, collective_id):
    rows, width = part.shape[0] // RING, part.shape[1]
    copies = 2 * REDUCE_COPIES + 1 + GATHER_COPIES + TOTAL_COPIES
    vmem, anywhere = pl.BlockSpec(memory_space=pltpu.VMEM), pl.BlockSpec(memory_space=pl.ANY)
    coded = spread_shape(rows, width)
    return pl.pallas_call(
        images_kernel,
        out_shape=(
            jax.ShapeDtypeStruct(coded.shape[3:], coded.dtype),
            jax.ShapeDtypeStruct((rows, width), F32),
            jax.ShapeDtypeStruct((width, width), F32),
        ),
        in_specs=[vmem, anywhere],
        out_specs=(vmem, vmem, vmem),
        scratch_shapes=[
            pltpu.VMEM((rows, width), F32),
            pltpu.VMEM((width, width), F32),
            pltpu.VMEM(coded.shape[3:], coded.dtype),
            pltpu.VMEM(coded.shape, coded.dtype),
            pltpu.VMEM(tile.shape, F32),
            pltpu.VMEM(part.shape, F32),
        ]
        + reduce_scratch(rows, width)
        + reduce_scratch(rows, width)
        + total_scratch(width)
        + [
            pltpu.SemaphoreType.DMA((copies,)),
            pltpu.SemaphoreType.DMA((copies,)),
            pltpu.SemaphoreType.DMA,
            pltpu.SemaphoreType.DMA,
        ],
        compiler_params=pltpu.CompilerParams(collective_id=collective_id, has_side_effects=True),
        name="images",
    )(part, tile)


def bases_kernel(scale, share_ref, own_ref, inverse_ref, rows_ref, total_ref, basis_ref, gram, *refs):
    scratch = refs[:7]
    send, recv = refs[7:]
    place = Place()
    links = Links(send, recv)
    meet(everyone(place))
    image = times_transpose(share_ref[...], inverse_ref[...])
    rows_ref[pl.ds(place.t, 1)] = image[None]
    gram[...] = gram_of(image)
    total = total_steps(gram, total_ref, scratch, links, place)
    next(total)
    next(total)
    own = rows_ref.at[place.t]
    around = [links.go(own, own, place.ahead("t", d)) for d in (1, -1)]
    basis_ref[...] = times_transpose(decode(own_ref[...]), inverse_ref[...], scale)
    next(total)
    next(total)
    next(total)
    half = image.shape[0] // 2
    onward = []
    for d, made in zip((1, -1), around):
        made.wait_recv()
        held = rows_ref.at[place.along("t", -d), pl.ds(0 if d > 0 else half, half)]
        onward.append(links.go(held, held, place.ahead("t", d)))
    run(total)
    for made in onward:
        made.wait_recv()
    settle(links, place)


def bases(share, own, inverse, scale, collective_id):
    rows, width = share.shape
    copies = TOTAL_COPIES + 4
    vmem = pl.BlockSpec(memory_space=pltpu.VMEM)
    out, total, basis = pl.pallas_call(
        functools.partial(bases_kernel, scale),
        out_shape=(
            jax.ShapeDtypeStruct((RING, rows, width), F32),
            jax.ShapeDtypeStruct((width, width), F32),
            jax.ShapeDtypeStruct((rows, width), F32),
        ),
        in_specs=[vmem] * 3,
        out_specs=(vmem, vmem, vmem),
        scratch_shapes=[pltpu.VMEM((width, width), F32)]
        + total_scratch(width)
        + [pltpu.SemaphoreType.DMA((copies,)), pltpu.SemaphoreType.DMA((copies,))],
        compiler_params=pltpu.CompilerParams(collective_id=collective_id, has_side_effects=True),
        name="bases",
    )(share, own, inverse)
    return out.reshape(-1, width), total, basis


def body(hidden, down_weight, covariance, keep_index, start_basis):
    total_tokens = TOK_DEV * lax.axis_size("fsdp")
    root = math.sqrt(D)
    mlp_out, start_codes, kept_rows, kept_cols = down_projection(
        hidden, down_weight, start_basis, keep_index, covariance.shape[1], 0
    )
    kept_rows = kept_rows.reshape(-1, kept_rows.shape[-1])
    kept_cols = kept_cols.reshape(-1, kept_cols.shape[-1])
    new_covariance, part_one = update_and_image(
        covariance, start_codes, kept_rows, kept_cols, 1.0 / total_tokens
    )
    own_codes, share_two, total_one = images(part_one, new_covariance, 1)
    inverse_one = inverse_factor(total_one)
    rows_two, total_two, first_basis = bases(share_two, own_codes, inverse_one, root, 2)
    final_basis = inverse_factor(total_two, rows_two, root)
    return (mlp_out, new_covariance, first_basis, final_basis)


def solution(mesh):
    placed = (
        P("tensor", "fsdp"),
        P("fsdp", "tensor"),
        P("tensor", "fsdp"),
        P("fsdp", None),
        P("fsdp", None),
    )
    return jax.shard_map(
        body,
        mesh=mesh,
        in_specs=placed,
        out_specs=(
            P("fsdp", "tensor"),
            P("tensor", "fsdp"),
            P(("tensor", "fsdp"), None),
            P("fsdp", None),
        ),
        check_vma=False,
    )
```
